128 devices in a mesh: gx: 8 (over z, core), gy: 4 (over x), gz: 4 (over y).
Axes of the slice: x: 4, y: 4, z: 4, core: 2. Of those that a mesh axis runs over, the one named last changes fastest.
Arguments:
- source_residual: float32 [64, 256, 1024], P('gz', 'gx', 'gy'), may hold values from -8 to 8
- storage: float32 [64, 256, 1024], P('gz', 'gx', 'gy'), may hold values from 0.05 to 3
- conductivity: float32 [64, 256, 1024], P('gz', 'gx', 'gy'), may hold values from 0.05 to 2
- primal_label: int32 [64, 256, 4], P('gz', 'gx', 'gy'), may hold values from 0 to 31
- zone_of_block: int32 [16384, 1], P(('gx', 'gy', 'gz')), may hold values from 0 to 127; in each aligned block of 128 rows (0 to 127, 128 to 255, ...) at most 4 rows name the same one
- coarse_factor: float32 [4096, 4096], P(('gx', 'gy', 'gz')), may hold values from -0.0009765625 to 0.0009765625
- zone_factor: bfloat16 [128, 256, 256], P(('gx', 'gy', 'gz')), may hold values from -0.375 to 0.375
Outputs:
- solution: float32 [64, 256, 1024], P('gz', 'gx', 'gy')
- residual: float32 [64, 256, 1024], P('gz', 'gx', 'gy')
The draws below stay inside these ranges and needn't reach their ends.
Inputs may be any that keep to these rules, and one draw needn't show every extreme that they name: `zone_of_block`: among the face blocks of one subdomain, no zone is named more than 4 times.
All inputs are finite; a program needn't handle non-finite values.
Results may differ from the reference program's by a relative error of at most 0.018.
Values may be sent and summed in bfloat16 or wider, within the bound.
No kernel may reach another device: no remote copies, remote signals or barrier semaphores. Data moves between devices by JAX's collectives and lax.ppermute only.
A program may use at most 64 MiB of HBM per device.

```python
import math
import jax
import jax.numpy as jnp
import numpy as np
from jax import lax

CZ = 16
CX = 32
CY = 256
FB = 256
KC = 32
INNER = 8
ITERS = 2
CAP = 4
NZ = 64
NX = 256
NY = 1024
ZONES = 128
NC = 4096
WB = 128
NBLK = 16384
N_GX = 8
N_GY = 4
N_GZ = 4


def draw_source_residual(key, part):
    depth_pos = jnp.arange(NZ, dtype=jnp.float32)[:, None, None] / NZ
    first_pos = jnp.arange(NX, dtype=jnp.float32)[None, :, None] / NX
    second_pos = jnp.arange(NY, dtype=jnp.float32)[None, None, :] / NY
    position_trend = (depth_pos + first_pos + second_pos) / 3.0
    amplitude = 0.5 + 1.5 * position_trend
    rough_part = jax.random.normal(key, (NZ, NX, NY), jnp.float32)
    values = amplitude * (0.7 + rough_part)
    return jnp.clip(values, -8.0, 8.0)


def place_ends(array, own_key, least, largest):
    shape = array.shape
    place = [jax.random.randint(jax.random.fold_in(own_key, axis), (), 0, shape[axis]) for axis in range(len(shape))]
    array = array.at[tuple(place)].set(least)
    longest = shape.index(max(shape))
    place[longest] = (place[longest] + 1) % shape[longest]
    return array.at[tuple(place)].set(largest)


def level_of(rng, extent, split, least, largest):
    gain = 1.0
    for position, parts in split:
        steps = jax.random.uniform(jax.random.fold_in(jax.random.fold_in(rng, 6), position), (parts,), jnp.float32, least / len(split), largest / len(split))
        gain = gain * jnp.repeat(jnp.exp(steps), extent[position] // parts).reshape((-1,) + (1,) * (len(extent) - 1 - position))
    return gain


def assign_block(key, own, number, rows, number_of, top, limit, slope):
    order = jax.random.permutation(key, number_of)
    packed, ordinary = shares(number_of, rows * top, limit, slope, True), shares(number_of, rows * top, limit, slope, False)
    places = jnp.arange(number_of)

    def named(lengths, offset_by):
        used = int((lengths > 0).sum())
        fixed = max(1, used // 4)
        passed = fixed + (places - fixed + offset_by * (used - fixed)) % max(1, number_of - fixed)
        return jnp.zeros((number_of,), jnp.int32).at[order[jnp.where(places < fixed, places, passed)]].set(jnp.asarray(lengths, jnp.int32))

    lengths = jnp.where(number % 4 == 0, named(packed, number // 4), named(ordinary, number - number // 4 - 1))
    mixed = jax.random.permutation(jax.random.fold_in(own, 3), number_of)
    donor, taker = mixed[0:number_of // 2 * 2:2], mixed[1:number_of // 2 * 2:2]
    slack = jnp.minimum(lengths[donor] - 1, limit - lengths[taker]) // 2
    slack = jnp.where((donor == order[0]) | (taker == order[0]) | (lengths[taker] == 0), 0, jnp.maximum(slack, 0))
    passed = jax.random.randint(jax.random.fold_in(own, 4), (number_of // 2,), 0, 1 << 20) % (slack + 1)
    lengths = lengths.at[donor].add(-passed).at[taker].add(passed)
    items = jnp.searchsorted(jnp.cumsum(lengths), jnp.arange(rows * top), side="right").astype(jnp.int32)
    listing = items.reshape(top, rows).T
    listing = listing[jax.random.permutation(jax.random.fold_in(own, 1), rows)]
    offset_by = jax.random.randint(jax.random.fold_in(own, 2), (rows, 1), 0, top)
    return jnp.take_along_axis(listing, (jnp.arange(top)[None, :] + offset_by) % top, axis=1)


def shares(amount, total, bound, slope, full):
    weights = [(1 << 20) // math.isqrt(rank ** slope) + 1 for rank in range(1, amount + 1)]
    largest = bound if full else min(bound, max(-(-total // amount), total * weights[0] // sum(weights)))
    least = 1 if total - largest >= amount - 1 else 0
    holding, spare = [largest] + [least] * (amount - 1), total - largest - least * (amount - 1)
    while spare > 0:
        movable = [i for i in range(1, amount) if holding[i] < largest] or [i for i in range(1, amount) if holding[i] < bound]
        pool, budget = sum([weights[i] for i in movable]), spare
        for i in movable:
            addition = min(bound - holding[i], max(1, budget * weights[i] // pool), spare)
            holding[i] = holding[i] + addition
            spare = spare - addition
    return np.array(holding)


def centred(stream_key, dims, scale, bound, pieces=(), held_as=jnp.bfloat16):
    level = level_of(stream_key, dims, pieces, -0.22, 0.18) if pieces else 1.0
    drawn = jax.random.normal(stream_key, dims, jnp.float32) * scale * level
    return jnp.minimum(jnp.maximum(drawn, -bound), bound).astype(held_as)


def setup_inputs(seed: int = 0) -> dict:
    keys = jax.random.split(jax.random.key(seed), 8)
    source_residual = draw_source_residual(jax.random.fold_in(keys[7], 71), 0)
    storage = jnp.clip(jnp.exp(math.log(3.0) - 4.0943445 * jax.random.uniform(keys[1], (NZ, NX, NY), jnp.float32) ** level_of(keys[1], (NZ, NX, NY), ((0, 4), (1, 8), (2, 4)), -0.2, 0.2)), 0.05, 3.0)
    conductivity = jnp.clip(jnp.exp(math.log(2.0) - 3.6888794 * jax.random.uniform(keys[2], (NZ, NX, NY), jnp.float32) ** level_of(keys[2], (NZ, NX, NY), ((0, 4), (1, 8), (2, 4)), -0.2, 0.2)), 0.05, 2.0)
    primal_label = place_ends(jax.random.randint(keys[3], (NZ, NX, NY // CY), 0, KC), jax.random.fold_in(keys[3], 1), 0, KC - 1).astype(jnp.int32)
    zone_of_block_keys = jax.random.split(jax.random.fold_in(keys[4], 1), NBLK // WB)
    zone_of_block_turns = jax.random.permutation(jax.random.fold_in(keys[4], 3), NBLK // WB)
    zone_of_block = jax.vmap(lambda own, number: assign_block(jax.random.fold_in(keys[4], 2), own, number, WB, ZONES, 1, CAP, 2))(zone_of_block_keys, zone_of_block_turns).reshape((NBLK, 1))
    coarse_factor = centred(keys[5], (NC, NC), (2 * NC * (CX * CY * CZ // KC)) ** -0.5, 0.0009765625, ((0, 128),), jnp.float32)
    zone_factor = centred(keys[6], (ZONES, FB, FB), FB ** -0.5, 0.375, ((0, 128),))
    return {"source_residual": source_residual, "storage": storage, "conductivity": conductivity, "primal_label": primal_label, "zone_of_block": zone_of_block, "coarse_factor": coarse_factor, "zone_factor": zone_factor}


HIGHEST = lax.Precision.HIGHEST


def to_blocks(field, span_y):
    shaped = field.reshape(N_GZ, CZ, N_GX, CX, N_GY, span_y)
    return shaped.transpose(2, 4, 0, 1, 3, 5).reshape(N_GX * N_GY * N_GZ, CZ, CX, span_y)


def from_blocks(field):
    shaped = field.reshape(N_GX, N_GY, N_GZ, CZ, CX, CY)
    return shaped.transpose(2, 3, 0, 4, 1, 5).reshape(NZ, NX, NY)


def face_conductances(padded, center):
    return (
        0.5 * (padded[2:, 1:-1, 1:-1] + center),
        0.5 * (padded[:-2, 1:-1, 1:-1] + center),
        0.5 * (padded[1:-1, 2:, 1:-1] + center),
        0.5 * (padded[1:-1, :-2, 1:-1] + center),
        0.5 * (padded[1:-1, 1:-1, 2:] + center),
        0.5 * (padded[1:-1, 1:-1, :-2] + center),
    )


def neighbour_sum(conductances, padded):
    summed = conductances[0] * padded[..., 2:, 1:-1, 1:-1] + conductances[1] * padded[..., :-2, 1:-1, 1:-1]
    summed = summed + conductances[2] * padded[..., 1:-1, 2:, 1:-1] + conductances[3] * padded[..., 1:-1, :-2, 1:-1]
    summed = summed + conductances[4] * padded[..., 1:-1, 1:-1, 2:] + conductances[5] * padded[..., 1:-1, 1:-1, :-2]
    return summed


def local_solve(rhs, conductances, diagonal):
    iterate = jnp.zeros_like(rhs)
    remain = rhs
    scaled = remain / diagonal
    search = scaled
    inner_rz = jnp.sum(remain * scaled, axis=(1, 2, 3), keepdims=True)
    for sweep_index in range(INNER):
        padded = jnp.pad(search, ((0, 0), (1, 1), (1, 1), (1, 1)))
        applied = diagonal * search - neighbour_sum(conductances, padded)
        step_size = inner_rz / jnp.sum(search * applied, axis=(1, 2, 3), keepdims=True)
        iterate = iterate + step_size * search
        remain = remain - step_size * applied
        scaled = remain / diagonal
        inner_next = jnp.sum(remain * scaled, axis=(1, 2, 3), keepdims=True)
        search = scaled + (inner_next / inner_rz) * search
        inner_rz = inner_next
    return iterate


def refine_term(field, zones, zone_factor):
    devices = field.shape[0]
    layers = jnp.concatenate([field[:, :2], field[:, -2:]], axis=1)
    blocks = layers.reshape(devices, -1, FB).astype(jnp.bfloat16)

    def one_device(block_pair):
        block_rows, zone_ids = block_pair
        chosen = zone_factor[zone_ids].astype(jnp.float32)
        lifted = jnp.einsum("bf,bfg->bg", block_rows.astype(jnp.float32), chosen).astype(jnp.bfloat16)
        return jnp.einsum("bg,bfg->bf", lifted.astype(jnp.float32), chosen).astype(jnp.bfloat16)

    refined = lax.map(one_device, (blocks, zones)).astype(jnp.float32)
    refined = refined.reshape(devices, 4, CX, CY)
    middle = jnp.zeros((devices, CZ - 4, CX, CY), jnp.float32)
    return jnp.concatenate([refined[:, :2], middle, refined[:, 2:]], axis=1)


def reference(source_residual, storage, conductivity, primal_label, zone_of_block, coarse_factor, zone_factor):
    devices = N_GX * N_GY * N_GZ
    conductances = face_conductances(jnp.pad(conductivity, 1), conductivity)
    diagonal = storage + conductances[0] + conductances[1] + conductances[2] + conductances[3] + conductances[4] + conductances[5]
    local_faces = tuple(to_blocks(single, CY) for single in conductances)
    local_diagonal = to_blocks(diagonal, CY)
    labels = to_blocks(primal_label, 1).reshape(devices, CZ * CX)
    onehot = (labels[:, :, None] == jnp.arange(KC, dtype=jnp.int32)[None, None, :]).astype(jnp.float32)
    zones = zone_of_block.reshape(devices, -1)

    def coarse_vector(blocked):
        line_values = jnp.sum(blocked, axis=3).reshape(devices, CZ * CX)
        restricted = jnp.einsum("dl,dlk->dk", line_values, onehot, precision=HIGHEST)
        return jnp.dot(restricted.reshape(-1), coarse_factor, precision=HIGHEST)

    def precondition(field):
        blocked = to_blocks(field, CY)
        summed = coarse_vector(blocked)
        coarse_coef = jnp.dot(coarse_factor, summed, precision=HIGHEST).reshape(devices, KC)
        line_values = jnp.einsum("dlk,dk->dl", onehot, coarse_coef, precision=HIGHEST).reshape(devices, CZ, CX, 1)
        local_part = local_solve(blocked, local_faces, local_diagonal)
        return from_blocks(local_part + line_values + refine_term(blocked, zones, zone_factor))

    solution = jnp.zeros_like(source_residual)
    residual = source_residual
    precond = precondition(residual)
    current_rz = jnp.sum(residual * precond)
    direction = precond
    for outer_step in range(ITERS):
        applied = diagonal * direction - neighbour_sum(conductances, jnp.pad(direction, 1))
        step_size = current_rz / jnp.sum(direction * applied)
        solution = solution + step_size * direction
        residual = residual - step_size * applied
        if outer_step + 1 < ITERS:
            precond = precondition(residual)
            next_rz = jnp.sum(residual * precond)
            direction = precond + (next_rz / current_rz) * direction
            current_rz = next_rz
    return solution, residual
```

```python
import jax
import jax.numpy as jnp
from jax import lax
from jax.experimental import pallas as pl
from jax.experimental.pallas import tpu as pltpu
from jax.sharding import PartitionSpec as P

CZ = 16
CX = 32
CY = 256
KC = 32
INNER = 8
CAP = 4
ZN = 128
FB = 256
LANES = 128
WIDE = CAP * FB
SEND = WIDE + 2 * LANES
AX = ("gx", "gy", "gz")
F32 = jnp.float32
BF16 = jnp.bfloat16

VMEM = pl.BlockSpec(memory_space=pltpu.VMEM)
SMEM = pl.BlockSpec(memory_space=pltpu.SMEM)


def sds(shape, dtype=F32):
    return jax.ShapeDtypeStruct(shape, dtype)


def call(body, outs, n_in, scratch=(), smem_in=()):
    return pl.pallas_call(
        body,
        out_shape=outs,
        in_specs=[SMEM if i in smem_in else VMEM for i in range(n_in)],
        out_specs=jax.tree.map(lambda _: VMEM, outs),
        scratch_shapes=scratch,
        compiler_params=pltpu.CompilerParams(vmem_limit_bytes=48 * 1024 * 1024),
    )


def iota(shape, dim):
    return lax.broadcasted_iota(jnp.int32, shape, dim)


def total(x):
    return jnp.sum(jnp.sum(x, axis=1, keepdims=True), axis=0, keepdims=True)


def fold(x):
    half = x[:, :LANES] + x[:, LANES:]
    return half[0:8] + half[8:16] + half[16:24] + half[24:32]


def split3(x):
    high = x.astype(BF16).astype(F32)
    rest = x - high
    mid = rest.astype(BF16).astype(F32)
    return high, mid, rest - mid


def face_store(plane_of, refs, xs_lo, xs_hi):
    zlo, zhi, xlo, xhi, ylo, yhi = refs
    lane = iota((CX, LANES), 1)
    acc_lo = jnp.zeros((CX, LANES), F32)
    acc_hi = jnp.zeros((CX, LANES), F32)
    for z in range(CZ):
        plane = plane_of(z)
        if z == 0:
            zlo[...] = plane.astype(BF16)
        if z == CZ - 1:
            zhi[...] = plane.astype(BF16)
        xs_lo[z : z + 1, :] = plane[0:1, :]
        xs_hi[z : z + 1, :] = plane[CX - 1 : CX, :]
        acc_lo = jnp.where(lane == z, plane[:, 0:1], acc_lo)
        acc_hi = jnp.where(lane == z, plane[:, CY - 1 : CY], acc_hi)
    xlo[...] = xs_lo[...].astype(BF16)
    xhi[...] = xs_hi[...].astype(BF16)
    ylo[...] = acc_lo.astype(BF16)
    yhi[...] = acc_hi.astype(BF16)


FACE_OUTS = (
    sds((CX, CY), BF16),
    sds((CX, CY), BF16),
    sds((CZ, CY), BF16),
    sds((CZ, CY), BF16),
    sds((CX, LANES), BF16),
    sds((CX, LANES), BF16),
)
FACE_SCRATCH = (pltpu.VMEM((CZ, CY), F32), pltpu.VMEM((CZ, CY), F32))


def exchange(faces):
    out = []
    for axis, (low, high) in zip(("gz", "gx", "gy"), (faces[0:2], faces[2:4], faces[4:6])):
        n = lax.axis_size(axis)
        forward = [(i, (i + 1) % n) for i in range(n)]
        backward = [((i + 1) % n, i) for i in range(n)]
        out.append(lax.ppermute(high, axis, forward))
        out.append(lax.ppermute(low, axis, backward))
    return out


def zone_tables(zrow, zcol):
    shape = (ZN, ZN)
    row = jnp.broadcast_to(zrow, shape)
    col = jnp.broadcast_to(zcol, shape)
    return row, col, row == col


def store_send(send, blocks, zrow, zcol, u_rows, scalars, tile):
    row, col, same = zone_tables(zrow, zcol)
    sub, lane = iota((ZN, ZN), 0), iota((ZN, ZN), 1)
    slot = jnp.sum(jnp.where(same & (sub < lane), 1.0, 0.0), axis=0, keepdims=True)
    hit = row == sub
    for k in range(CAP):
        put = jnp.where(hit & (jnp.broadcast_to(slot, (ZN, ZN)) == float(k)), 1.0, 0.0)
        send[:, k * FB : (k + 1) * FB] = jnp.dot(
            put.astype(BF16), blocks, preferred_element_type=F32
        ).astype(BF16)
    high = u_rows.astype(BF16).astype(F32)
    tile[0:32, :] = high
    tile[32:64, :] = u_rows - high
    tile[64:128, :] = jnp.zeros((64, LANES), F32)
    for i, value in enumerate(scalars):
        for j, piece in enumerate(split3(value)):
            at = 64 + 3 * i + j
            tile[at : at + 1, :] = jnp.broadcast_to(piece, (1, LANES))
    send[:, WIDE : WIDE + LANES] = tile[...].T.astype(BF16)
    send[:, WIDE + LANES :] = jnp.zeros((ZN, LANES), BF16)


def coarse_rows(line_of, label, factor, rows):
    lane = iota((CX, LANES), 1)
    sub = iota((CX, LANES), 0)
    acc = jnp.zeros((CX, LANES), F32)
    for z in range(CZ):
        acc = acc + jnp.where(label[z] == lane, line_of(z), 0.0)
    g_row = jnp.broadcast_to(jnp.sum(acc, axis=0, keepdims=True), (CX, LANES))
    g_col = jnp.sum(jnp.where(sub == lane, g_row, 0.0), axis=1, keepdims=True)
    g = jnp.broadcast_to(g_col, (KC, LANES))
    for t in range(32):
        rows[t : t + 1, :] = jnp.sum(
            factor[:, t * LANES : (t + 1) * LANES] * g, axis=0, keepdims=True
        )
    return rows[...]


def face_blocks(field):
    return jnp.concatenate([field[0], field[1], field[CZ - 2], field[CZ - 1]], axis=0).astype(BF16)


def faces_body(k, *refs):
    face_store(lambda z: k[z], refs[:6], *refs[6:])


def pack_body(r, label, zrow, zcol, factor, send, tile, rows):
    u_rows = coarse_rows(
        lambda z: jnp.sum(r[z], axis=1, keepdims=True), label, factor, rows
    )
    store_send(send, face_blocks(r), zrow[...], zcol[...], u_rows, (), tile)


def lift_store(out, x_of, tail, zone):
    factor = zone[0]
    for k in range(CAP):
        lifted = jnp.dot(x_of(k), factor, preferred_element_type=F32).astype(BF16)
        back = lax.dot_general(
            lifted, factor, (((1,), (1,)), ((), ())), preferred_element_type=F32
        )
        out[:, k * FB : (k + 1) * FB] = back.astype(BF16)
    lane = iota((1, LANES), 1)
    u = jnp.where(lane < 32, tail + pltpu.roll(tail, LANES - 32, 1), 0.0)
    high = u.astype(BF16).astype(F32)
    both = high + pltpu.roll(u - high, 32, 1)
    out[:, WIDE : WIDE + LANES] = jnp.broadcast_to(both, (ZN, LANES)).astype(BF16)
    out[:, WIDE + LANES :] = jnp.zeros((ZN, LANES), BF16)


def tail_sum(got):
    return jnp.sum(got[:, WIDE : WIDE + LANES].astype(F32), axis=0, keepdims=True)


def lift0_body(got, zone, out):
    lift_store(out, lambda k: got[:, k * FB : (k + 1) * FB], tail_sum(got), zone)


def lift1_body(got0, got1, zone, out, scalars):
    tail0, tail1 = tail_sum(got0), tail_sum(got1)
    lane = iota((1, LANES), 1)

    def scalar(i):
        keep = (lane >= 64 + 3 * i) & (lane < 67 + 3 * i)
        return jnp.sum(jnp.where(keep, tail1, 0.0), axis=1, keepdims=True)

    rz, curvature = scalar(0), scalar(1)
    alpha = rz / curvature

    def x_of(k):
        old = got0[:, k * FB : (k + 1) * FB].astype(F32)
        new = got1[:, k * FB : (k + 1) * FB].astype(F32)
        return (old - alpha * new).astype(BF16)

    lift_store(out, x_of, tail0 - alpha * tail1, zone)
    scalars[0:1, :] = jnp.broadcast_to(alpha, (1, LANES))
    scalars[1:2, :] = jnp.broadcast_to(rz, (1, LANES))
    scalars[2:3, :] = jnp.broadcast_to(curvature, (1, LANES))
    scalars[3:8, :] = jnp.zeros((5, LANES), F32)


def minus_neighbours(p, below, above, cz_below, cz_above, cx, cy):
    tx = cx * p
    ty = cy * p
    out = p - cx * pltpu.roll(p, CX - 1, 0) - pltpu.roll(tx, 1, 0)
    out = out - cy * pltpu.roll(p, CY - 1, 1) - pltpu.roll(ty, 1, 1)
    if below is not None:
        out = out - cz_below * below
    if above is not None:
        out = out - cz_above * above
    return out


def cg(cz, cx, cy, p, q, e, y, rho):
    def step(_, carry):
        rho, beta = carry
        acc = jnp.zeros((8, LANES), F32)
        below, now = None, q[0] + beta * p[0]
        p[0] = now
        for z in range(CZ):
            above = None
            if z + 1 < CZ:
                above = q[z + 1] + beta * p[z + 1]
                p[z + 1] = above
            image = minus_neighbours(
                now,
                below,
                above,
                cz[z - 1] if z else None,
                cz[z] if z + 1 < CZ else None,
                cx[z],
                cy[z],
            )
            e[z] = image
            acc = acc + fold(now * image)
            below, now = now, above
        a = rho / total(acc)
        acc = jnp.zeros((8, LANES), F32)
        for z in range(CZ):
            y[z] = y[z] + a * p[z]
            left = q[z] - a * e[z]
            q[z] = left
            acc = acc + fold(left * left)
        new = total(acc)
        return new, new / rho

    lax.fori_loop(0, INNER, step, (rho, jnp.zeros((1, 1), F32)))


def start_cg(r_of, s, p, q, y):
    acc = jnp.zeros((8, LANES), F32)
    for z in range(CZ):
        left = s[z] * r_of(z)
        q[z] = left
        p[z] = jnp.zeros((CX, CY), F32)
        y[z] = jnp.zeros((CX, CY), F32)
        acc = acc + fold(left * left)
    return total(acc)


def solve0_body(
    flags, k, storage, r, kzl, kzh, kxl, kxh, kyl, kyh,
    local, s, sinv, cz, cx, cy, bzl, bzh, bxl, bxh, byl, byh,
    p, q, e, y,
):
    sub, lane = iota((CX, CY), 0), iota((CX, CY), 1)
    zl, zh = flags[0] * kzl[...].astype(F32), flags[1] * kzh[...].astype(F32)
    xl, xh = flags[2] * kxl[...].astype(F32), flags[3] * kxh[...].astype(F32)
    yl, yh = flags[4] * kyl[...].astype(F32), flags[5] * kyh[...].astype(F32)
    bzl[...] = flags[0] * 0.5 * (k[0] + zl)
    bzh[...] = flags[1] * 0.5 * (k[CZ - 1] + zh)
    lane_half = iota((CX, LANES), 1)
    y_edge_lo = jnp.zeros((CX, LANES), F32)
    y_edge_hi = jnp.zeros((CX, LANES), F32)
    for z in range(CZ):
        c = k[z]
        x_row_lo, x_row_hi = xl[z : z + 1, :], xh[z : z + 1, :]
        bxl[z : z + 1, :] = flags[2] * 0.5 * (c[0:1, :] + x_row_lo)
        bxh[z : z + 1, :] = flags[3] * 0.5 * (c[CX - 1 : CX, :] + x_row_hi)
        y_edge_lo = jnp.where(lane_half == z, c[:, 0:1], y_edge_lo)
        y_edge_hi = jnp.where(lane_half == z, c[:, CY - 1 : CY], y_edge_hi)
        around = (k[z - 1] if z else zl) + (k[z + 1] if z + 1 < CZ else zh)
        right = pltpu.roll(c, CX - 1, 0)
        around = around + jnp.where(sub == CX - 1, x_row_hi, right)
        around = around + jnp.where(sub == 0, x_row_lo, pltpu.roll(c, 1, 0))
        ahead = pltpu.roll(c, CY - 1, 1)
        end = pltpu.roll(yh, LANES - 1 - z, 1)
        around = around + jnp.where(lane == CY - 1, jnp.concatenate([end, end], axis=1), ahead)
        begin = pltpu.roll(yl, (LANES - z) % LANES, 1)
        around = around + jnp.where(
            lane == 0, jnp.concatenate([begin, begin], axis=1), pltpu.roll(c, 1, 1)
        )
        diagonal = storage[z] + 3.0 * c + 0.5 * around
        root = lax.rsqrt(diagonal)
        root = root * (1.5 - 0.5 * diagonal * root * root)
        s[z] = root
        sinv[z] = diagonal * root
        cx[z] = jnp.where(sub == CX - 1, 0.0, 0.5 * (c + right) * root * pltpu.roll(root, CX - 1, 0))
        cy[z] = jnp.where(lane == CY - 1, 0.0, 0.5 * (c + ahead) * root * pltpu.roll(root, CY - 1, 1))
        if z:
            cz[z - 1] = 0.5 * (k[z - 1] + c) * s[z - 1] * root
    cz[CZ - 1] = jnp.zeros((CX, CY), F32)
    byl[...] = flags[4] * 0.5 * (y_edge_lo + yl)
    byh[...] = flags[5] * 0.5 * (y_edge_hi + yh)
    rho = start_cg(lambda z: r[z], s, p, q, y)
    cg(cz, cx, cy, p, q, e, y, rho)
    for z in range(CZ):
        local[z] = s[z] * y[z]


def solve1_body(scalars, r, image, s, cz, cx, cy, local, p, q, e, y):
    alpha = scalars[0:1, 0:1]
    rho = start_cg(lambda z: r[z] - alpha * image[z], s, p, q, y)
    cg(cz, cx, cy, p, q, e, y, rho)
    for z in range(CZ):
        local[z] = s[z] * y[z]


def combine_body(local, got, label, zcol, zrow, factor, out, *refs):
    lane, sub = iota((CX, LANES), 1), iota((CX, LANES), 0)
    flipped = got[:, WIDE : WIDE + LANES].astype(F32).T
    u = flipped[0:32, :] + flipped[32:64, :]
    acc = jnp.zeros((KC, LANES), F32)
    for t in range(32):
        acc = acc + factor[:, t * LANES : (t + 1) * LANES] * u[t : t + 1, :]
    coef_col = jnp.sum(acc, axis=1, keepdims=True)
    coef = jnp.sum(jnp.where(sub == lane, coef_col, 0.0), axis=0, keepdims=True)
    coef = jnp.broadcast_to(coef, (CX, LANES))
    row, col, same = zone_tables(zrow[...], zcol[...])
    zsub, zlane = iota((ZN, ZN), 0), iota((ZN, ZN), 1)
    slot = jnp.sum(jnp.where(same & (zlane < zsub), 1.0, 0.0), axis=1, keepdims=True)
    slot = jnp.broadcast_to(slot, (ZN, ZN))
    placed = jnp.zeros((ZN, FB), F32)
    for k in range(CAP):
        take = jnp.where((col == zlane) & (slot == float(k)), 1.0, 0.0).astype(BF16)
        placed = placed + jnp.dot(
            take, got[:, k * FB : (k + 1) * FB], preferred_element_type=F32
        )
    order = {0: 0, 1: 1, CZ - 2: 2, CZ - 1: 3}
    for z in range(CZ):
        value = jnp.sum(jnp.where(label[z] == lane, coef, 0.0), axis=1, keepdims=True)
        plane = local[z] + value
        if z in order:
            at = order[z] * CX
            plane = plane + placed[at : at + CX, :]
        out[z] = plane
    face_store(lambda z: out[z], refs[:6], *refs[6:])


def apply_plane(z, v, sinv, cz, cx, cy, bounds, halos, masks):
    bzl, bzh, bxl, bxh, byl, byh = bounds
    hzl, hzh, hxl, hxh, hyl, hyh = halos
    first_row, last_row, first_lane, last_lane = masks
    inverse = sinv[z]
    scaled = minus_neighbours(
        v[z] * inverse,
        v[z - 1] * sinv[z - 1] if z else None,
        v[z + 1] * sinv[z + 1] if z + 1 < CZ else None,
        cz[z - 1] if z else None,
        cz[z] if z + 1 < CZ else None,
        cx[z],
        cy[z],
    )
    out = scaled * inverse
    out = out - jnp.where(first_row, bxl[z : z + 1, :] * hxl[z : z + 1, :], 0.0)
    out = out - jnp.where(last_row, bxh[z : z + 1, :] * hxh[z : z + 1, :], 0.0)
    low = pltpu.roll(byl * hyl, (LANES - z) % LANES, 1)
    high = pltpu.roll(byh * hyh, LANES - 1 - z, 1)
    out = out - jnp.where(first_lane, jnp.concatenate([low, low], axis=1), 0.0)
    out = out - jnp.where(last_lane, jnp.concatenate([high, high], axis=1), 0.0)
    if z == 0:
        out = out - bzl[...] * hzl
    if z == CZ - 1:
        out = out - bzh[...] * hzh
    return out


def apply_inputs(bound_refs, halo_refs):
    bzl, bzh, bxl, bxh, byl, byh = bound_refs
    halos = [h[...].astype(F32) for h in halo_refs]
    bounds = (bzl, bzh, bxl[...], bxh[...], byl[...], byh[...])
    sub, lane = iota((CX, CY), 0), iota((CX, CY), 1)
    return bounds, halos, (sub == 0, sub == CX - 1, lane == 0, lane == CY - 1)


def apply0_body(v, r, sinv, cz, cx, cy, *refs):
    bounds, halos, masks = apply_inputs(refs[0:6], refs[6:12])
    label, zrow, zcol, factor, image, send, tile, rows = refs[12:]
    rz = jnp.zeros((8, LANES), F32)
    curvature = jnp.zeros((8, LANES), F32)
    lines = []
    for z in range(CZ):
        out = apply_plane(z, v, sinv, cz, cx, cy, bounds, halos, masks)
        image[z] = out
        lines.append(jnp.sum(out, axis=1, keepdims=True))
        rz = rz + fold(r[z] * v[z])
        curvature = curvature + fold(v[z] * out)
    u_rows = coarse_rows(lambda z: lines[z], label, factor, rows)
    store_send(
        send, face_blocks(image), zrow[...], zcol[...], u_rows, (total(rz), total(curvature)), tile
    )


def apply1_body(scalars, v, r, image0, sinv, cz, cx, cy, *refs):
    bounds, halos, masks = apply_inputs(refs[0:6], refs[6:12])
    image, sums = refs[12:]
    alpha = scalars[0:1, 0:1]
    sums3 = [jnp.zeros((8, LANES), F32) for _ in range(3)]
    for z in range(CZ):
        out = apply_plane(z, v, sinv, cz, cx, cy, bounds, halos, masks)
        image[z] = out
        at = v[z]
        sums3[0] = sums3[0] + fold((r[z] - alpha * image0[z]) * at)
        sums3[1] = sums3[1] + fold(at * out)
        sums3[2] = sums3[2] + fold(at * image0[z])
    lane = iota((ZN, LANES), 1)
    row = jnp.zeros((ZN, LANES), F32)
    for i in range(3):
        row = jnp.where(lane == i, total(sums3[i]), row)
    sums[...] = row


def final_body(scalars, got, v, d, r, image0, image1, solution, residual):
    sums = jnp.sum(got[...], axis=0, keepdims=True)
    alpha0, rz0, curvature0 = scalars[0:1, 0:1], scalars[1:2, 0:1], scalars[2:3, 0:1]
    rz1, vav, vad = sums[:, 0:1], sums[:, 1:2], sums[:, 2:3]
    beta = rz1 / rz0
    alpha1 = rz1 / (vav + 2.0 * beta * vad + beta * beta * curvature0)
    mix = alpha0 + alpha1 * beta
    for z in range(CZ):
        solution[z] = mix * d[z] + alpha1 * v[z]
        residual[z] = r[z] - mix * image0[z] - alpha1 * image1[z]


FIELD = sds((CZ, CX, CY))
FIELD_SCRATCH = pltpu.VMEM((CZ, CX, CY), F32)
BOUND_OUTS = (
    sds((CX, CY)),
    sds((CX, CY)),
    sds((CZ, CY)),
    sds((CZ, CY)),
    sds((CX, LANES)),
    sds((CX, LANES)),
)
PACKED = sds((ZN, SEND), BF16)
TILE = pltpu.VMEM((LANES, LANES), F32)
ROWS = pltpu.VMEM((KC, LANES), F32)


def swap(x):
    return lax.all_to_all(x, AX, split_axis=0, concat_axis=0, tiled=True)


def per_device(r, storage, k, label, zone_of_block, factor, zone_factor):
    zcol = zone_of_block
    zrow = zone_of_block.reshape(1, ZN)
    flags = jnp.stack(
        [
            (lax.axis_index(axis) != edge).astype(F32)
            for axis in ("gz", "gx", "gy")
            for edge in (0, lax.axis_size(axis) - 1)
        ]
    )
    k_faces = call(faces_body, FACE_OUTS, 1, FACE_SCRATCH)(k)
    send0 = call(pack_body, PACKED, 5, (TILE, ROWS))(r, label, zrow, zcol, factor)
    got0 = swap(send0)
    k_halos = exchange(k_faces)
    back0 = swap(call(lift0_body, PACKED, 2)(got0, zone_factor))
    local, s, sinv, cz, cx, cy, *bounds = call(
        solve0_body, (FIELD,) * 6 + BOUND_OUTS, 10, (FIELD_SCRATCH,) * 4, (0,)
    )(flags, k, storage, r, *k_halos)

    def combine(local, back):
        z, *faces = call(combine_body, (FIELD,) + FACE_OUTS, 6, FACE_SCRATCH)(
            local, back, label, zcol, zrow, factor
        )
        return z, exchange(faces)

    d, halos = combine(local, back0)
    image0, send1 = call(apply0_body, (FIELD, PACKED), 22, (TILE, ROWS))(
        d, r, sinv, cz, cx, cy, *bounds, *halos, label, zrow, zcol, factor
    )
    got1 = swap(send1)
    back1, scalars = call(lift1_body, (PACKED, sds((8, LANES))), 3)(got0, got1, zone_factor)
    back1 = swap(back1)
    local = call(solve1_body, FIELD, 7, (FIELD_SCRATCH,) * 4)(scalars, r, image0, s, cz, cx, cy)
    v, halos = combine(local, back1)
    image1, sums = call(apply1_body, (FIELD, sds((ZN, LANES))), 20)(
        scalars, v, r, image0, sinv, cz, cx, cy, *bounds, *halos
    )
    return call(final_body, (FIELD, FIELD), 7)(scalars, swap(sums), v, d, r, image0, image1)


def solution(mesh):
    field = P("gz", "gx", "gy")
    in_specs = (field, field, field, field, P(AX, None), P(AX, None), P(AX, None, None))
    return jax.shard_map(
        per_device, mesh=mesh, in_specs=in_specs, out_specs=(field, field), check_vma=False
    )
```

```python
import jax
import jax.numpy as jnp
from jax import lax
from jax.experimental import pallas as pl
from jax.experimental.pallas import tpu as pltpu
from jax.sharding import PartitionSpec as P

CZ = 16
CX = 32
CY = 256
KC = 32
INNER = 8
CAP = 4
ZN = 128
FB = 256
EXTRA = 2 * CAP
PARTS = EXTRA + 2
LANES = 128
AX = ("gx", "gy", "gz")
F32 = jnp.float32
BF16 = jnp.bfloat16

def sds(shape, dtype=F32):
    return jax.ShapeDtypeStruct(shape, dtype)


class Load:
    def __init__(self, source, buffer, sems, chunks):
        self.buffer = buffer
        self.size = buffer.shape[0] // chunks
        self.copies = []
        for i in range(chunks):
            part = pl.ds(i * self.size, self.size)
            self.copies.append(
                pltpu.make_async_copy(source.at[part], buffer.at[part], sems.at[i])
            )

    def start(self, i):
        self.copies[i].start()

    def wait(self, i):
        if self.copies[i] is not None:
            self.copies[i].wait()
            self.copies[i] = None

    def full(self):
        for i in range(len(self.copies)):
            self.wait(i)
        return self.buffer

    def __getitem__(self, z):
        self.wait(z // self.size)
        return self.buffer[z]


class Store:
    def __init__(self, target, buffer, sems, chunks):
        self.buffer, self.target, self.sems = buffer, target, sems
        self.size = buffer.shape[0] // chunks
        self.copies = [None] * chunks

    def flush(self, i):
        part = pl.ds(i * self.size, self.size)
        copy = pltpu.make_async_copy(self.buffer.at[part], self.target.at[part], self.sems.at[i])
        copy.start()
        self.copies[i] = copy

    def __setitem__(self, z, value):
        self.buffer[z] = value
        if z % self.size == self.size - 1:
            self.flush(z // self.size)

    def __getitem__(self, z):
        return self.buffer[z]

    def send(self):
        for i, copy in enumerate(self.copies):
            if copy is None:
                self.flush(i)

    def finish(self):
        self.send()
        for copy in self.copies:
            copy.wait()


SPACE = {"a": pl.ANY, "o": pltpu.HBM, "s": pltpu.SMEM, "v": pltpu.VMEM, "h": pltpu.HBM, "c": pltpu.HBM, "p": pltpu.HBM}
COPIED = "hcpa"
CHUNKS = 4


def spec(mode):
    return pl.BlockSpec(memory_space=SPACE[mode])


def run(body, ins, outs, scratch=(), mixed=()):
    moved = [(m, a) for side in (ins, outs) for m, a in side if m in COPIED]
    n_chunks = [1 if m in "ha" else CHUNKS for m, _ in moved]
    buffers = [pltpu.VMEM(a.shape, a.dtype) for m, a in moved if m != "p"]
    sems = [pltpu.SemaphoreType.DMA((n,)) for n in n_chunks]
    passed = [sds(a.shape, a.dtype) for m, a in ins if m == "p"]
    n_in, n_out, n_pass, n_own = len(ins), len(outs), len(passed), len(scratch)

    def kernel(*refs):
        refs = list(refs)

        def take(n):
            head = refs[:n]
            del refs[:n]
            return head

        in_refs, out_refs, pass_refs, own = take(n_in), take(n_out), take(n_pass), take(n_own)
        bufs = take(len(buffers))
        given, made, loads, stores = [], [], [], []
        for (m, _), ref in zip(ins, in_refs):
            if m in COPIED:
                buf = pass_refs.pop(0) if m == "p" else bufs.pop(0)
                given.append(Load(ref, buf, refs.pop(0), 1 if m in "ha" else CHUNKS))
                loads.append(given[-1])
            else:
                given.append(ref)
        for (m, _), ref in zip(outs, out_refs):
            if m in COPIED:
                made.append(Store(ref, bufs.pop(0), refs.pop(0), 1 if m in "ha" else CHUNKS))
                stores.append(made[-1])
            else:
                made.append(ref)
        groups = {id(given[g[0]]): [given[i] for i in g] for g in mixed}
        joined = [id(given[i]) for g in mixed for i in g]
        for x in loads:
            for i in range(len(x.copies)):
                if id(x) not in joined:
                    x.start(i)
                for one in groups.get(id(x), ()):
                    one.start(i)
        body(given, made, *own)
        for x in stores:
            x.send()
        for x in loads:
            x.full()
        for x in stores:
            x.finish()

    return pl.pallas_call(
        kernel,
        out_shape=tuple(
            pltpu.HBM(a.shape, a.dtype) if m in "hco" else a for m, a in outs
        )
        + tuple(passed),
        in_specs=[spec(m) for m, _ in ins],
        out_specs=tuple(spec(m) for m, _ in outs) + (spec("v"),) * n_pass,
        scratch_shapes=tuple(scratch) + tuple(buffers) + tuple(sems),
        compiler_params=pltpu.CompilerParams(vmem_limit_bytes=24 * 1024 * 1024),
    )(*[pltpu.with_memory_space_constraint(a, pltpu.HBM) if m in "hcp" else a for m, a in ins])


def full(x):
    return x.full() if isinstance(x, Load) else x


def raw(x):
    return x.buffer if isinstance(x, (Load, Store)) else x


def iota(shape, dim):
    return lax.broadcasted_iota(jnp.int32, shape, dim)


def total(x):
    return jnp.sum(jnp.sum(x, axis=1, keepdims=True), axis=0, keepdims=True)


def fold(x):
    half = x[:, :LANES] + x[:, LANES:]
    return half[0:8] + half[8:16] + half[16:24] + half[24:32]


def split3(x):
    high = x.astype(BF16).astype(F32)
    rest = x - high
    mid = rest.astype(BF16).astype(F32)
    return high, mid, rest - mid


def face_store(plane_of, refs, xs_lo, xs_hi):
    zlo, zhi, xlo, xhi, ylo, yhi = (raw(x) for x in refs)
    lane = iota((CX, LANES), 1)
    acc_lo = jnp.zeros((CX, LANES), F32)
    acc_hi = jnp.zeros((CX, LANES), F32)
    for z in range(CZ):
        plane = plane_of(z)
        if z == 0:
            zlo[...] = plane.astype(BF16)
        if z == CZ - 1:
            zhi[...] = plane.astype(BF16)
        xs_lo[z : z + 1, :] = plane[0:1, :]
        xs_hi[z : z + 1, :] = plane[CX - 1 : CX, :]
        acc_lo = jnp.where(lane == z, plane[:, 0:1], acc_lo)
        acc_hi = jnp.where(lane == z, plane[:, CY - 1 : CY], acc_hi)
    xlo[...] = xs_lo[...].astype(BF16)
    xhi[...] = xs_hi[...].astype(BF16)
    ylo[...] = acc_lo.astype(BF16)
    yhi[...] = acc_hi.astype(BF16)


FACE_OUTS = (
    sds((CX, CY), BF16),
    sds((CX, CY), BF16),
    sds((CZ, CY), BF16),
    sds((CZ, CY), BF16),
    sds((CX, LANES), BF16),
    sds((CX, LANES), BF16),
)
FACE_SCRATCH = (pltpu.VMEM((CZ, CY), F32), pltpu.VMEM((CZ, CY), F32))


def exchange(faces):
    out = []
    for axis, (low, high) in zip(("gz", "gx", "gy"), (faces[0:2], faces[2:4], faces[4:6])):
        n = lax.axis_size(axis)
        forward = [(i, (i + 1) % n) for i in range(n)]
        backward = [((i + 1) % n, i) for i in range(n)]
        out.append(lax.ppermute(high, axis, forward))
        out.append(lax.ppermute(low, axis, backward))
    return out


def slots(zrow):
    shape = (ZN, ZN)
    sub, lane = iota(shape, 0), iota(shape, 1)
    row = jnp.broadcast_to(zrow, shape)
    zcol = jnp.sum(jnp.where(sub == lane, row, 0), axis=1, keepdims=True)
    same = row == zcol
    slot_row = jnp.sum(jnp.where(same & (sub < lane), 1, 0), axis=0, keepdims=True)
    slot_col = jnp.sum(jnp.where(same & (lane < sub), 1, 0), axis=1, keepdims=True)
    return zrow + ZN * slot_row, zcol + ZN * slot_col


def part_rows(part, first=0, count=ZN):
    return pl.ds(first * PARTS + part, count, stride=PARTS)


def store_send(send, blocks, zrow, u_rows, scalars, tile, wide):
    key, _ = slots(zrow)
    put = jnp.where(iota((CAP * ZN, ZN), 0) == key, 1.0, 0.0).astype(BF16)
    placed = jnp.dot(put, blocks, preferred_element_type=F32)
    for k in range(CAP):
        rows = placed[k * ZN : (k + 1) * ZN, :]
        wide[part_rows(k), :] = rows[:, :LANES]
        wide[part_rows(CAP + k), :] = rows[:, LANES:]
    high = u_rows.astype(BF16).astype(F32)
    tile[0:32, :] = high
    tile[32:64, :] = u_rows - high
    tile[64:128, :] = jnp.zeros((64, LANES), F32)
    for i, value in enumerate(scalars):
        for j, piece in enumerate(split3(value)):
            at = 64 + 3 * i + j
            tile[at : at + 1, :] = jnp.broadcast_to(piece, (1, LANES))
    wide[part_rows(EXTRA), :] = tile[...].T
    wide[part_rows(EXTRA + 1), :] = jnp.zeros((ZN, LANES), F32)
    send[...] = wide[...].astype(BF16)


def label_columns(label, tile):
    tile[...] = jnp.zeros((LANES, LANES), F32)
    tile[0:CZ, 0:CX] = full(label)[...].astype(F32)
    return tile[...].T[0:CX, :]


def coarse_rows(line_of, columns, factor, rows):
    lane = iota((CX, LANES), 1)
    kind = lane.astype(F32)
    sub = iota((CX, LANES), 0)
    acc = jnp.zeros((CX, LANES), F32)
    for z in range(CZ):
        acc = acc + jnp.where(columns[:, z : z + 1] == kind, line_of(z), 0.0)
    g_row = jnp.broadcast_to(jnp.sum(acc, axis=0, keepdims=True), (CX, LANES))
    g_col = jnp.sum(jnp.where(sub == lane, g_row, 0.0), axis=1, keepdims=True)
    g = jnp.broadcast_to(g_col, (KC, LANES))
    factor = full(factor)
    for t in range(32):
        rows[t : t + 1, :] = jnp.sum(
            factor[:, t * LANES : (t + 1) * LANES] * g, axis=0, keepdims=True
        )
    return rows[...]


def face_blocks(field):
    return jnp.concatenate([field[0], field[1], field[CZ - 2], field[CZ - 1]], axis=0).astype(BF16)


def pack_body(ins, outs, tile, rows, wide, xs_lo, xs_hi):
    label, zrow, r, factor, k = ins
    send, *faces = outs
    columns = label_columns(label, tile)
    u_rows = coarse_rows(
        lambda z: jnp.sum(r[z], axis=1, keepdims=True), columns, factor, rows
    )
    store_send(raw(send), face_blocks(r), full(zrow)[...], u_rows, (), tile, wide)
    send.send()
    face_store(lambda z: k[z], faces, xs_lo, xs_hi)


def lift_store(out, wide, tail, zone):
    factor = zone[0]
    lane = iota((1, LANES), 1)
    u = jnp.where(lane < 32, tail + pltpu.roll(tail, LANES - 32, 1), 0.0)
    high = u.astype(BF16).astype(F32)
    both = high + pltpu.roll(u - high, 32, 1)
    size = ZN // CHUNKS
    for i in range(CHUNKS):
        at = i * size
        x = jnp.concatenate(
            [
                jnp.concatenate(
                    [wide[part_rows(k, at, size), :], wide[part_rows(CAP + k, at, size), :]],
                    axis=1,
                )
                for k in range(CAP)
            ],
            axis=0,
        ).astype(BF16)
        lifted = jnp.dot(x, factor, preferred_element_type=F32).astype(BF16)
        back = lax.dot_general(
            lifted, factor, (((1,), (1,)), ((), ())), preferred_element_type=F32
        )
        for k in range(CAP):
            rows = back[k * size : (k + 1) * size, :]
            wide[part_rows(k, at, size), :] = rows[:, :LANES]
            wide[part_rows(CAP + k, at, size), :] = rows[:, LANES:]
        wide[part_rows(EXTRA, at, size), :] = jnp.broadcast_to(both, (size, LANES))
        part = slice(at * PARTS, (at + size) * PARTS)
        out.buffer[part, :] = wide[part, :].astype(BF16)
        out.flush(i)


def tail_sum(wide):
    return jnp.sum(wide[part_rows(EXTRA), :], axis=0, keepdims=True)


def lift0_body(ins, outs, wide, sem):
    got, zone = ins
    out, kept = outs
    keep = pltpu.make_async_copy(got, kept, sem)
    keep.start()
    wide[...] = got[...].astype(F32)
    lift_store(out, wide, tail_sum(wide), full(zone))
    keep.wait()


def lift1_body(ins, outs, wide):
    zone, got0, got1 = ins
    out, scalars = outs
    store, scalars = scalars, raw(scalars)
    wide[...] = got1[...].astype(F32)
    tail1 = tail_sum(wide)
    lane = iota((1, LANES), 1)

    def scalar(i):
        keep = (lane >= 64 + 3 * i) & (lane < 67 + 3 * i)
        return jnp.sum(jnp.where(keep, tail1, 0.0), axis=1, keepdims=True)

    rz, curvature = scalar(0), scalar(1)
    alpha = rz / curvature
    scalars[0:1, :] = jnp.broadcast_to(alpha, (1, LANES))
    scalars[1:2, :] = jnp.broadcast_to(rz, (1, LANES))
    scalars[2:3, :] = jnp.broadcast_to(curvature, (1, LANES))
    scalars[3:8, :] = jnp.zeros((5, LANES), F32)
    store.send()
    wide[...] = full(got0)[...].astype(F32) - alpha * wide[...]
    lift_store(out, wide, tail_sum(wide), full(zone))


def minus_neighbours(p, below, above, cz_below, cz_above, cx, cy):
    tx = cx * p
    ty = cy * p
    out = p - cx * pltpu.roll(p, CX - 1, 0) - pltpu.roll(tx, 1, 0)
    out = out - cy * pltpu.roll(p, CY - 1, 1) - pltpu.roll(ty, 1, 1)
    if below is not None:
        out = out - cz_below * below
    if above is not None:
        out = out - cz_above * above
    return out


def apply_scaled(p_of, cz, cx, cy, e):
    acc = jnp.zeros((8, LANES), F32)
    below, now = None, p_of(0)
    for z in range(CZ):
        above = p_of(z + 1) if z + 1 < CZ else None
        image = minus_neighbours(
            now,
            below,
            above,
            cz[z - 1] if z else None,
            cz[z] if z + 1 < CZ else None,
            cx[z],
            cy[z],
        )
        e[z] = image
        acc = acc + fold(now * image)
        below, now = now, above
    return total(acc)


def cg(cz, cx, cy, s, p, q, e, y, rho, local):
    def first_of(z):
        p[z] = q[z]
        return q[z]

    a = rho / apply_scaled(first_of, cz, cx, cy, e)

    def move(a, started):
        acc = jnp.zeros((8, LANES), F32)
        for z in range(CZ):
            y[z] = y[z] + a * p[z] if started else a * p[z]
            left = q[z] - a * e[z]
            q[z] = left
            acc = acc + fold(left * left)
        return total(acc)

    new = move(a, False)
    carry = (new, new / rho)
    cz, cx, cy = raw(cz), raw(cx), raw(cy)

    def advance(beta):
        def next_of(z):
            value = q[z] + beta * p[z]
            p[z] = value
            return value

        return apply_scaled(next_of, cz, cx, cy, e)

    def step(_, carry):
        rho, beta = carry
        new = move(rho / advance(beta), True)
        return new, new / rho

    rho, beta = lax.fori_loop(0, INNER - 2, step, carry)
    a = rho / advance(beta)
    for z in range(CZ):
        local[z] = s[z] * (y[z] + a * p[z])


def start_cg(r_of, s, q):
    acc = jnp.zeros((8, LANES), F32)
    for z in range(CZ):
        left = s[z] * r_of(z)
        q[z] = left
        acc = acc + fold(left * left)
    return total(acc)


def solve0_body(ins, outs, p, q, e, y):
    flags, *halos, k, storage, r = ins
    local, s, sinv, cz, cx, cy, bounds_zx, bounds_y = outs
    kzl, kzh, kxl, kxh, kyl, kyh = (full(h) for h in halos)
    zx, by = raw(bounds_zx), raw(bounds_y)
    sub, lane = iota((CX, CY), 0), iota((CX, CY), 1)
    zl, zh = flags[0] * kzl[...].astype(F32), flags[1] * kzh[...].astype(F32)
    xl, xh = flags[2] * kxl[...].astype(F32), flags[3] * kxh[...].astype(F32)
    yl, yh = flags[4] * kyl[...].astype(F32), flags[5] * kyh[...].astype(F32)
    zx[0:32, :] = flags[0] * 0.5 * (k[0] + zl)
    zx[32:64, :] = flags[1] * 0.5 * (k[CZ - 1] + zh)
    lane_half = iota((CX, LANES), 1)
    y_edge_lo = jnp.zeros((CX, LANES), F32)
    y_edge_hi = jnp.zeros((CX, LANES), F32)
    for z in range(CZ):
        c = k[z]
        x_row_lo, x_row_hi = xl[z : z + 1, :], xh[z : z + 1, :]
        zx[64 + z : 65 + z, :] = flags[2] * 0.5 * (c[0:1, :] + x_row_lo)
        zx[80 + z : 81 + z, :] = flags[3] * 0.5 * (c[CX - 1 : CX, :] + x_row_hi)
        y_edge_lo = jnp.where(lane_half == z, c[:, 0:1], y_edge_lo)
        y_edge_hi = jnp.where(lane_half == z, c[:, CY - 1 : CY], y_edge_hi)
        around = (k[z - 1] if z else zl) + (k[z + 1] if z + 1 < CZ else zh)
        right = pltpu.roll(c, CX - 1, 0)
        around = around + jnp.where(sub == CX - 1, x_row_hi, right)
        around = around + jnp.where(sub == 0, x_row_lo, pltpu.roll(c, 1, 0))
        ahead = pltpu.roll(c, CY - 1, 1)
        end = pltpu.roll(yh, LANES - 1 - z, 1)
        around = around + jnp.where(lane == CY - 1, jnp.concatenate([end, end], axis=1), ahead)
        begin = pltpu.roll(yl, (LANES - z) % LANES, 1)
        around = around + jnp.where(
            lane == 0, jnp.concatenate([begin, begin], axis=1), pltpu.roll(c, 1, 1)
        )
        diagonal = storage[z] + 3.0 * c + 0.5 * around
        root = lax.rsqrt(diagonal)
        root = root * (1.5 - 0.5 * diagonal * root * root)
        s[z] = root
        sinv[z] = diagonal * root
        cx[z] = jnp.where(sub == CX - 1, 0.0, 0.5 * (c + right) * root * pltpu.roll(root, CX - 1, 0))
        cy[z] = jnp.where(lane == CY - 1, 0.0, 0.5 * (c + ahead) * root * pltpu.roll(root, CY - 1, 1))
        if z:
            cz[z - 1] = 0.5 * (k[z - 1] + c) * s[z - 1] * root
    cz[CZ - 1] = jnp.zeros((CX, CY), F32)
    by[0:32, :] = flags[4] * 0.5 * (y_edge_lo + yl)
    by[32:64, :] = flags[5] * 0.5 * (y_edge_hi + yh)
    bounds_zx.send()
    bounds_y.send()
    rho = start_cg(lambda z: r[z], s, q)
    cg(raw(cz), raw(cx), raw(cy), raw(s), p, q, e, y, rho, local)


def solve1_body(ins, outs, p, q, e, y):
    scalars, r, image, s, cz, cx, cy = ins
    (local,) = outs
    alpha = full(scalars)[0:1, 0:1]
    rho = start_cg(lambda z: r[z] - alpha * image[z], s, q)
    cg(cz, cx, cy, raw(s), p, q, e, y, rho, local)


def combine_body(ins, outs, xs_lo, xs_hi, tile, wide, sems):
    got, zrow, label, factor, local, *_ = ins
    out, kept, *faces = outs
    lane, sub = iota((CX, LANES), 1), iota((CX, LANES), 0)
    wide[...] = got[...].astype(F32)
    _, key = slots(full(zrow)[...])
    columns = label_columns(label, tile)
    factor = full(factor)
    flipped = wide[part_rows(EXTRA), :].T
    u = flipped[0:32, :] + flipped[32:64, :]
    acc = jnp.zeros((KC, LANES), F32)
    for t in range(32):
        acc = acc + factor[:, t * LANES : (t + 1) * LANES] * u[t : t + 1, :]
    coef_col = jnp.sum(acc, axis=1, keepdims=True)
    coef = jnp.sum(jnp.where(sub == lane, coef_col, 0.0), axis=0, keepdims=True)
    coef = jnp.broadcast_to(coef, (CX, LANES))
    back = jnp.concatenate(
        [
            jnp.concatenate([wide[part_rows(k), :], wide[part_rows(CAP + k), :]], axis=1)
            for k in range(CAP)
        ],
        axis=0,
    ).astype(BF16)
    take = jnp.where(iota((ZN, CAP * ZN), 1) == key, 1.0, 0.0).astype(BF16)
    placed = jnp.dot(take, back, preferred_element_type=F32)
    kind = lane.astype(F32)
    order = {0: 0, 1: 1, CZ - 2: 2, CZ - 1: 3}
    for z in range(CZ):
        value = jnp.sum(
            jnp.where(columns[:, z : z + 1] == kind, coef, 0.0), axis=1, keepdims=True
        )
        plane = local[z] + value
        if z in order:
            at = order[z] * CX
            plane = plane + placed[at : at + CX, :]
        out[z] = plane
    keep = pltpu.make_async_copy(out, kept, sems)
    keep.start()
    face_store(lambda z: out[z], faces, xs_lo, xs_hi)
    keep.wait()


def apply_plane(z, v, sinv, cz, cx, cy, bounds, halos, masks):
    bzl, bzh, bxl, bxh, byl, byh = bounds
    hzl, hzh, hxl, hxh, hyl, hyh = halos
    first_row, last_row, first_lane, last_lane = masks
    inverse = sinv[z]
    scaled = minus_neighbours(
        v[z] * inverse,
        v[z - 1] * sinv[z - 1] if z else None,
        v[z + 1] * sinv[z + 1] if z + 1 < CZ else None,
        cz[z - 1] if z else None,
        cz[z] if z + 1 < CZ else None,
        cx[z],
        cy[z],
    )
    out = scaled * inverse
    out = out - jnp.where(first_row, bxl[z : z + 1, :] * hxl[z : z + 1, :], 0.0)
    out = out - jnp.where(last_row, bxh[z : z + 1, :] * hxh[z : z + 1, :], 0.0)
    low = pltpu.roll(byl * hyl, (LANES - z) % LANES, 1)
    high = pltpu.roll(byh * hyh, LANES - 1 - z, 1)
    out = out - jnp.where(first_lane, jnp.concatenate([low, low], axis=1), 0.0)
    out = out - jnp.where(last_lane, jnp.concatenate([high, high], axis=1), 0.0)
    if z == 0:
        out = out - bzl * hzl
    if z == CZ - 1:
        out = out - bzh * hzh
    return out


def apply_inputs(zx, by, halo_refs):
    halos = [full(h)[...].astype(F32) for h in halo_refs]
    zx, by = full(zx), full(by)
    bounds = (zx[0:32, :], zx[32:64, :], zx[64:80, :], zx[80:96, :], by[0:32, :], by[32:64, :])
    sub, lane = iota((CX, CY), 0), iota((CX, CY), 1)
    return bounds, halos, (sub == 0, sub == CX - 1, lane == 0, lane == CY - 1)


def apply0_body(ins, outs, tile, rows, wide):
    v, sinv, cz, cx, cy, zx, by, r, *halo_refs, label, zrow, factor = ins
    image, send = outs
    bounds, halos, masks = apply_inputs(zx, by, halo_refs)
    rz = jnp.zeros((8, LANES), F32)
    curvature = jnp.zeros((8, LANES), F32)
    lines = []
    for z in range(CZ):
        out = apply_plane(z, v, sinv, cz, cx, cy, bounds, halos, masks)
        image[z] = out
        lines.append(jnp.sum(out, axis=1, keepdims=True))
        rz = rz + fold(r[z] * v[z])
        curvature = curvature + fold(v[z] * out)
    columns = label_columns(label, tile)
    u_rows = coarse_rows(lambda z: lines[z], columns, factor, rows)
    sums = (total(rz), total(curvature))
    store_send(raw(send), face_blocks(image), full(zrow)[...], u_rows, sums, tile, wide)


def apply1_body(ins, outs):
    v, sinv, cz, cx, cy, zx, by, r, image0, *halo_refs, scalars = ins
    image, sums = outs
    bounds, halos, masks = apply_inputs(zx, by, halo_refs)
    alpha = full(scalars)[0:1, 0:1]
    sums3 = [jnp.zeros((8, LANES), F32) for _ in range(3)]
    for z in range(CZ):
        out = apply_plane(z, v, sinv, cz, cx, cy, bounds, halos, masks)
        image[z] = out
        at = v[z]
        sums3[0] = sums3[0] + fold((r[z] - alpha * image0[z]) * at)
        sums3[1] = sums3[1] + fold(at * out)
        sums3[2] = sums3[2] + fold(at * image0[z])
    lane = iota((ZN, LANES), 1)
    row = jnp.zeros((ZN, LANES), F32)
    for i in range(3):
        row = jnp.where(lane == i, total(sums3[i]), row)
    sums[...] = row


def final_body(ins, outs):
    scalars, got, d, v, r, image0, image1 = ins
    solution, residual = outs
    scalars = full(scalars)
    sums = jnp.sum(got[...], axis=0, keepdims=True)
    alpha0, rz0, curvature0 = scalars[0:1, 0:1], scalars[1:2, 0:1], scalars[2:3, 0:1]
    rz1, vav, vad = sums[:, 0:1], sums[:, 1:2], sums[:, 2:3]
    beta = rz1 / rz0
    alpha1 = rz1 / (vav + 2.0 * beta * vad + beta * beta * curvature0)
    mix = alpha0 + alpha1 * beta
    for z in range(CZ):
        solution[z] = mix * d[z] + alpha1 * v[z]
        residual[z] = r[z] - mix * image0[z] - alpha1 * image1[z]


FIELD = sds((CZ, CX, CY))
FIELD_SCRATCH = pltpu.VMEM((CZ, CX, CY), F32)
PACKED = sds((ZN * PARTS, LANES), BF16)
WIDE = pltpu.VMEM((ZN * PARTS, LANES), F32)
TILE = pltpu.VMEM((LANES, LANES), F32)
ROWS = pltpu.VMEM((KC, LANES), F32)


def swap(x):
    return lax.all_to_all(x, AX, split_axis=0, concat_axis=0, tiled=True)


def swap_packed(x):
    return swap(x.reshape(ZN, PARTS // 2, 2, LANES)).reshape(ZN * PARTS, LANES)


def each(mode, *arrays):
    return [(mode, a) for a in arrays]


def per_device(r, storage, k, label, zone_of_block, factor, zone_factor):
    zrow = zone_of_block.reshape(1, ZN)
    label = label.reshape(CZ, CX)
    flags = jnp.stack(
        [
            (lax.axis_index(axis) != edge).astype(F32)
            for axis in ("gz", "gx", "gy")
            for edge in (0, lax.axis_size(axis) - 1)
        ]
    )
    send0, *k_faces = run(
        pack_body,
        each("h", label, zrow) + each("c", r) + each("h", factor) + each("c", k),
        each("h", PACKED, *FACE_OUTS),
        (TILE, ROWS, WIDE) + FACE_SCRATCH,
    )
    got0 = swap_packed(send0)
    k_halos = exchange(k_faces)
    got0, *k_halos = lax.optimization_barrier((got0, *k_halos))
    back0, got0 = run(
        lift0_body,
        each("v", got0) + each("h", zone_factor),
        each("c", PACKED) + each("o", PACKED),
        (WIDE, pltpu.SemaphoreType.DMA),
    )
    back0 = swap_packed(back0)
    local, s, sinv, cz, cx, cy, *bounds = run(
        solve0_body,
        each("s", flags) + each("a", *k_halos) + each("c", k, storage, r),
        each("c", *(FIELD,) * 6) + each("h", sds((96, CY)), sds((64, LANES))),
        (FIELD_SCRATCH,) * 4,
        ((7, 8, 9),),
    )
    matrix = (sinv, cz, cx, cy, *bounds)

    def combine(local, back, more):
        field, kept, *rest = run(
            combine_body,
            each("v", back)
            + each("h", zrow, label, factor)
            + each("c", local)
            + each("p", *matrix, *more),
            each("v", FIELD) + each("o", FIELD) + each("v", *FACE_OUTS),
            FACE_SCRATCH + (TILE, WIDE, pltpu.SemaphoreType.DMA),
        )
        return field, kept, exchange(rest[:6]), rest[6:]

    field, d, halos, passed = combine(local, back0, (r,))
    image0, send1 = run(
        apply0_body,
        each("v", field, *passed, *halos) + each("h", label, zrow, factor),
        each("c", FIELD) + each("h", PACKED),
        (TILE, ROWS, WIDE),
    )
    got1 = swap_packed(send1)
    back1, scalars = run(
        lift1_body,
        each("h", zone_factor, got0) + each("v", got1),
        each("c", PACKED) + each("h", sds((8, LANES))),
        (WIDE,),
    )
    back1 = swap_packed(back1)
    (local,) = run(
        solve1_body,
        each("h", scalars) + each("c", r, image0, s, cz, cx, cy),
        each("c", FIELD),
        (FIELD_SCRATCH,) * 4,
        ((1, 2, 3), (4, 5, 6)),
    )
    field, v, halos, passed = combine(local, back1, (r, image0))
    image1, sums = run(
        apply1_body,
        each("v", field, *passed, *halos) + each("h", scalars),
        each("c", FIELD) + each("v", sds((ZN, LANES))),
    )
    return run(
        final_body,
        each("h", scalars) + each("v", swap(sums)) + each("c", d, v, r, image0, image1),
        each("c", FIELD, FIELD),
        (),
        ((2, 3, 4, 5, 6),),
    )


def solution(mesh):
    field = P("gz", "gx", "gy")
    in_specs = (field, field, field, field, P(AX, None), P(AX, None), P(AX, None, None))
    return jax.shard_map(
        per_device, mesh=mesh, in_specs=in_specs, out_specs=(field, field), check_vma=False
    )
```

```python
import jax
import jax.numpy as jnp
from jax import lax
from jax.experimental import pallas as pl
from jax.experimental.pallas import tpu as pltpu
from jax.sharding import PartitionSpec as P

CZ = 16
CX = 32
CY = 256
KC = 32
INNER = 8
CAP = 4
ZN = 128
FB = 256
EXTRA = 2 * CAP
PARTS = EXTRA + 2
LANES = 128
LINES = CZ * CX
AX = ("gx", "gy", "gz")
F32 = jnp.float32
BF16 = jnp.bfloat16

def sds(shape, dtype=F32):
    return jax.ShapeDtypeStruct(shape, dtype)


class Load:
    def __init__(self, source, buffer, sems, chunks):
        self.buffer = buffer
        self.size = buffer.shape[0] // chunks
        self.copies = []
        for i in range(chunks):
            part = pl.ds(i * self.size, self.size)
            self.copies.append(
                pltpu.make_async_copy(source.at[part], buffer.at[part], sems.at[i])
            )

    def start(self, i):
        self.copies[i].start()

    def wait(self, i):
        if self.copies[i] is not None:
            self.copies[i].wait()
            self.copies[i] = None

    def full(self):
        for i in range(len(self.copies)):
            self.wait(i)
        return self.buffer

    def __getitem__(self, z):
        self.wait(z // self.size)
        return self.buffer[z]


class Store:
    def __init__(self, target, buffer, sems, chunks):
        self.buffer, self.target, self.sems = buffer, target, sems
        self.size = buffer.shape[0] // chunks
        self.copies = [None] * chunks

    def flush(self, i):
        part = pl.ds(i * self.size, self.size)
        copy = pltpu.make_async_copy(self.buffer.at[part], self.target.at[part], self.sems.at[i])
        copy.start()
        self.copies[i] = copy

    def __setitem__(self, z, value):
        self.buffer[z] = value
        if z % self.size == self.size - 1:
            self.flush(z // self.size)

    def __getitem__(self, z):
        return self.buffer[z]

    def send(self):
        for i, copy in enumerate(self.copies):
            if copy is None:
                self.flush(i)

    def finish(self):
        self.send()
        for copy in self.copies:
            copy.wait()


SPACE = {"a": pl.ANY, "o": pltpu.HBM, "s": pltpu.SMEM, "v": pltpu.VMEM, "h": pltpu.HBM, "c": pltpu.HBM, "p": pltpu.HBM}
COPIED = "hcpa"
CHUNKS = 4


def chunks_of(mode, array):
    return CHUNKS if mode in "cp" and array.shape[0] > 8 else 1


def spec(mode):
    return pl.BlockSpec(memory_space=SPACE[mode])


def run(body, ins, outs, scratch=(), mixed=()):
    moved = [(m, a) for side in (ins, outs) for m, a in side if m in COPIED]
    n_chunks = [chunks_of(m, a) for m, a in moved]
    buffers = [pltpu.VMEM(a.shape, a.dtype) for m, a in moved if m != "p"]
    sems = [pltpu.SemaphoreType.DMA((n,)) for n in n_chunks]
    passed = [sds(a.shape, a.dtype) for m, a in ins if m == "p"]
    n_in, n_out, n_pass, n_own = len(ins), len(outs), len(passed), len(scratch)

    def kernel(*refs):
        refs = list(refs)

        def take(n):
            head = refs[:n]
            del refs[:n]
            return head

        in_refs, out_refs, pass_refs, own = take(n_in), take(n_out), take(n_pass), take(n_own)
        bufs = take(len(buffers))
        given, made, loads, stores = [], [], [], []
        for (m, _), ref in zip(ins, in_refs):
            if m in COPIED:
                buf = pass_refs.pop(0) if m == "p" else bufs.pop(0)
                given.append(Load(ref, buf, refs.pop(0), chunks_of(m, buf)))
                loads.append(given[-1])
            else:
                given.append(ref)
        for (m, _), ref in zip(outs, out_refs):
            if m in COPIED:
                made.append(Store(ref, bufs[0], refs.pop(0), chunks_of(m, bufs.pop(0))))
                stores.append(made[-1])
            else:
                made.append(ref)
        groups = {id(given[g[0]]): [given[i] for i in g] for g in mixed}
        joined = [id(given[i]) for g in mixed for i in g]
        for x in loads:
            for i in range(len(x.copies)):
                if id(x) not in joined:
                    x.start(i)
                for one in groups.get(id(x), ()):
                    one.start(i)
        body(given, made, *own)
        for x in stores:
            x.send()
        for x in loads:
            x.full()
        for x in stores:
            x.finish()

    return pl.pallas_call(
        kernel,
        out_shape=tuple(
            pltpu.HBM(a.shape, a.dtype) if m in "hco" else a for m, a in outs
        )
        + tuple(passed),
        in_specs=[spec(m) for m, _ in ins],
        out_specs=tuple(spec(m) for m, _ in outs) + (spec("v"),) * n_pass,
        scratch_shapes=tuple(scratch) + tuple(buffers) + tuple(sems),
        compiler_params=pltpu.CompilerParams(vmem_limit_bytes=24 * 1024 * 1024),
    )(*[pltpu.with_memory_space_constraint(a, pltpu.HBM) if m in "hcp" else a for m, a in ins])


def full(x):
    return x.full() if isinstance(x, Load) else x


def raw(x):
    return x.buffer if isinstance(x, (Load, Store)) else x


def iota(shape, dim):
    return lax.broadcasted_iota(jnp.int32, shape, dim)


def total(x):
    return jnp.sum(jnp.sum(x, axis=1, keepdims=True), axis=0, keepdims=True)


def fold(x):
    half = x[:, :LANES] + x[:, LANES:]
    return half[0:8] + half[8:16] + half[16:24] + half[24:32]


def split3(x):
    high = x.astype(BF16).astype(F32)
    rest = x - high
    mid = rest.astype(BF16).astype(F32)
    return high, mid, rest - mid


def choose(even, first, second):
    return even * first + (1.0 - even) * second


def edge_rows(flat):
    shape = (8, CY)
    sub, lane = iota(shape, 0), iota(shape, 1)
    hit = ((sub == 0) & (lane == 0)) | ((sub == 1) & (lane == CY - 1))
    pick = jnp.where(hit, 1.0, 0.0).astype(BF16)
    return lax.dot_general(pick, flat, (((1,), (1,)), ((), ())), preferred_element_type=F32)


def edge_field(rows):
    high, mid, low = split3(rows)
    sub = iota(rows.shape, 0)
    stack = jnp.where(
        sub < 2, high, jnp.where(sub < 4, pltpu.roll(mid, 2, 0), pltpu.roll(low, 4, 0))
    )
    shape = (8, CY)
    sub, lane = iota(shape, 0), iota(shape, 1)
    hit = ((sub % 2 == 0) & (lane == 0)) | ((sub % 2 == 1) & (lane == CY - 1))
    put = jnp.where(hit & (sub < 6), 1.0, 0.0).astype(BF16)
    stack = jnp.where(iota(rows.shape, 0) < 6, stack, 0.0)
    return jnp.dot(stack.T.astype(BF16), put, preferred_element_type=F32)


def face_store(plane_of, flags, refs, xs_lo, xs_hi):
    za, zb, xa, xb, ys = (raw(x) for x in refs)
    low, high = plane_of(0), plane_of(CZ - 1)
    za[...] = choose(flags[6], high, low).astype(BF16)
    zb[...] = choose(flags[6], low, high).astype(BF16)
    planes = []
    for z in range(CZ):
        plane = plane_of(z)
        xs_lo[z : z + 1, :] = plane[0:1, :]
        xs_hi[z : z + 1, :] = plane[CX - 1 : CX, :]
        planes.append(plane.astype(BF16))
    xa[...] = choose(flags[7], xs_hi[...], xs_lo[...]).astype(BF16)
    xb[...] = choose(flags[7], xs_lo[...], xs_hi[...]).astype(BF16)
    ys[...] = edge_rows(jnp.concatenate(planes, axis=0)).astype(BF16)


FACE_OUTS = (
    sds((CX, CY), BF16),
    sds((CX, CY), BF16),
    sds((CZ, CY), BF16),
    sds((CZ, CY), BF16),
    sds((8, LINES), BF16),
)
FACE_SCRATCH = (pltpu.VMEM((CZ, CY), F32), pltpu.VMEM((CZ, CY), F32))


def exchange(faces):
    za, zb, xa, xb, ys = faces
    out = []
    for axis, first, second in (("gz", za, zb), ("gx", xa, xb), ("gy", ys, ys)):
        n = lax.axis_size(axis)
        out.append(lax.ppermute(first, axis, [(i, i ^ 1) for i in range(n)]))
        out.append(
            lax.ppermute(second, axis, [(i, (i + 1 if i % 2 else i - 1) % n) for i in range(n)])
        )
    return out


def halo_values(flags, got):
    za, zb, xa, xb, ya, yb = (full(x)[...].astype(F32) for x in got)
    low, high = choose(flags[8], yb, ya), choose(flags[8], ya, yb)
    shape = (8, LINES)
    sub = iota(shape, 0)
    rows = jnp.where(
        sub == 0,
        jnp.broadcast_to(low[1:2, :], shape),
        jnp.where(sub == 1, jnp.broadcast_to(high[0:1, :], shape), 0.0),
    )
    return (
        choose(flags[6], zb, za),
        choose(flags[6], za, zb),
        choose(flags[7], xb, xa),
        choose(flags[7], xa, xb),
        rows,
    )


def slots(zrow):
    shape = (ZN, ZN)
    sub, lane = iota(shape, 0), iota(shape, 1)
    row = jnp.broadcast_to(zrow, shape)
    zcol = jnp.sum(jnp.where(sub == lane, row, 0), axis=1, keepdims=True)
    same = row == zcol
    slot_row = jnp.sum(jnp.where(same & (sub < lane), 1, 0), axis=0, keepdims=True)
    slot_col = jnp.sum(jnp.where(same & (lane < sub), 1, 0), axis=1, keepdims=True)
    return zrow + ZN * slot_row, zcol + ZN * slot_col


def part_rows(part, first=0, count=ZN):
    return pl.ds(first * PARTS + part, count, stride=PARTS)


def zone_hits(zrow):
    row, col = slots(zrow)
    put = jnp.where(iota((CAP * ZN, ZN), 0) == row, 1.0, 0.0).astype(BF16)
    take = jnp.where(iota((ZN, CAP * ZN), 1) == col, 1.0, 0.0).astype(BF16)
    return put, take


def store_send(send, blocks, put, u_rows, scalars, tile, wide):
    placed = jnp.dot(put, blocks, preferred_element_type=F32)
    for k in range(CAP):
        rows = placed[k * ZN : (k + 1) * ZN, :]
        wide[part_rows(k), :] = rows[:, :LANES]
        wide[part_rows(CAP + k), :] = rows[:, LANES:]
    high = u_rows.astype(BF16).astype(F32)
    tile[0:32, :] = high
    tile[32:64, :] = u_rows - high
    tile[64:128, :] = jnp.zeros((64, LANES), F32)
    for i, value in enumerate(scalars):
        for j, piece in enumerate(split3(value)):
            at = 64 + 3 * i + j
            tile[at : at + 1, :] = jnp.broadcast_to(piece, (1, LANES))
    wide[part_rows(EXTRA), :] = tile[...].T
    wide[part_rows(EXTRA + 1), :] = jnp.zeros((ZN, LANES), F32)
    send[...] = wide[...].astype(BF16)


def label_hits(label, tile, hits):
    tile[...] = jnp.zeros((LANES, LANES), F32)
    tile[0:CZ, 0:CX] = full(label)[...].astype(F32)
    columns = tile[...].T[0:CX, :]
    lane = iota((CX, LANES), 1)
    kind = jnp.where(lane < 3 * KC, lane % KC, -1).astype(F32)
    for z in range(CZ):
        hit = jnp.where(columns[:, z : z + 1] == kind, 1.0, 0.0)
        hits[z * CX : (z + 1) * CX, :] = hit.astype(BF16)


def coarse_rows(line_of, hits, factor, rows):
    lane = iota((CX, LANES), 1)
    sub = iota((CX, LANES), 0)
    acc = jnp.zeros((CX, LANES), F32)
    for z in range(CZ):
        acc = acc + hits[z * CX : (z + 1) * CX, :].astype(F32) * line_of(z)
    g_row = jnp.broadcast_to(jnp.sum(acc, axis=0, keepdims=True), (CX, LANES))
    g_col = jnp.sum(jnp.where(sub == lane, g_row, 0.0), axis=1, keepdims=True)
    g = jnp.broadcast_to(g_col, (KC, LANES))
    factor = full(factor)
    for t in range(32):
        rows[t : t + 1, :] = jnp.sum(
            factor[:, t * LANES : (t + 1) * LANES] * g, axis=0, keepdims=True
        )
    return rows[...]


def face_blocks(field):
    return jnp.concatenate([field[0], field[1], field[CZ - 2], field[CZ - 1]], axis=0).astype(BF16)


def pack_body(ins, outs, tile, rows, wide, xs_lo, xs_hi):
    flags, label, zrow, r, factor, k = ins
    send, hits, put, take, *faces = outs
    label_hits(label, tile, raw(hits))
    raw(put)[...], raw(take)[...] = zone_hits(full(zrow)[...])
    for x in (hits, put, take):
        x.send()
    u_rows = coarse_rows(
        lambda z: jnp.sum(r[z], axis=1, keepdims=True), raw(hits), factor, rows
    )
    store_send(raw(send), face_blocks(r), raw(put)[...], u_rows, (), tile, wide)
    send.send()
    face_store(lambda z: k[z], flags, faces, xs_lo, xs_hi)


def lift_store(out, wide, tail, zone):
    factor = zone[0]
    lane = iota((1, LANES), 1)
    u = jnp.where(lane < 32, tail + pltpu.roll(tail, LANES - 32, 1), 0.0)
    high = u.astype(BF16).astype(F32)
    both = high + pltpu.roll(u - high, 32, 1)
    size = ZN // CHUNKS
    for i in range(CHUNKS):
        at = i * size
        x = jnp.concatenate(
            [
                jnp.concatenate(
                    [wide[part_rows(k, at, size), :], wide[part_rows(CAP + k, at, size), :]],
                    axis=1,
                )
                for k in range(CAP)
            ],
            axis=0,
        ).astype(BF16)
        lifted = jnp.dot(x, factor, preferred_element_type=F32).astype(BF16)
        back = lax.dot_general(
            lifted, factor, (((1,), (1,)), ((), ())), preferred_element_type=F32
        )
        for k in range(CAP):
            rows = back[k * size : (k + 1) * size, :]
            wide[part_rows(k, at, size), :] = rows[:, :LANES]
            wide[part_rows(CAP + k, at, size), :] = rows[:, LANES:]
        wide[part_rows(EXTRA, at, size), :] = jnp.broadcast_to(both, (size, LANES))
        part = slice(at * PARTS, (at + size) * PARTS)
        out.buffer[part, :] = wide[part, :].astype(BF16)
        out.flush(i)


def tail_sum(wide):
    return jnp.sum(wide[part_rows(EXTRA), :], axis=0, keepdims=True)


def lift0_body(ins, outs, wide, sem):
    got, zone = ins
    out, kept = outs
    keep = pltpu.make_async_copy(got, kept, sem)
    keep.start()
    wide[...] = got[...].astype(F32)
    lift_store(out, wide, tail_sum(wide), full(zone))
    keep.wait()


def lift1_body(ins, outs, wide):
    zone, got0, got1 = ins
    out, scalars = outs
    store, scalars = scalars, raw(scalars)
    wide[...] = got1[...].astype(F32)
    tail1 = tail_sum(wide)
    lane = iota((1, LANES), 1)

    def scalar(i):
        keep = (lane >= 64 + 3 * i) & (lane < 67 + 3 * i)
        return jnp.sum(jnp.where(keep, tail1, 0.0), axis=1, keepdims=True)

    rz, curvature = scalar(0), scalar(1)
    alpha = rz / curvature
    scalars[0:1, :] = jnp.broadcast_to(alpha, (1, LANES))
    scalars[1:2, :] = jnp.broadcast_to(rz, (1, LANES))
    scalars[2:3, :] = jnp.broadcast_to(curvature, (1, LANES))
    scalars[3:8, :] = jnp.zeros((5, LANES), F32)
    store.send()
    wide[...] = full(got0)[...].astype(F32) - alpha * wide[...]
    lift_store(out, wide, tail_sum(wide), full(zone))


def minus_neighbours(p, below, above, cz_below, cz_above, cx, cy):
    tx = cx * p
    ty = cy * p
    out = p - cx * pltpu.roll(p, CX - 1, 0) - pltpu.roll(tx, 1, 0)
    out = out - cy * pltpu.roll(p, CY - 1, 1) - pltpu.roll(ty, 1, 1)
    if below is not None:
        out = out - cz_below * below
    if above is not None:
        out = out - cz_above * above
    return out


def cg(cz, cx, cy, s, p, q, e, y, first, local):
    def sweep(next_of, cz, cx, cy):
        rho = jnp.zeros((8, LANES), F32)
        pe, ee = rho, rho
        below, (now, left) = None, next_of(0)
        for z in range(CZ):
            rho = rho + fold(left * left)
            above = None
            if z + 1 < CZ:
                above, left = next_of(z + 1)
            image = minus_neighbours(
                now,
                below,
                above,
                cz[z - 1] if z else None,
                cz[z] if z + 1 < CZ else None,
                cx[z],
                cy[z],
            )
            e[z] = image
            pe = pe + fold(now * image)
            ee = ee + fold(image * image)
            below, now = now, above
        rho, pe, ee = total(rho), total(pe), total(ee)
        a = rho / pe
        return a, a * a * ee / rho - 1.0

    def begin(z):
        value = first(z)
        q[z] = value
        p[z] = value
        return value, value

    def second(a, beta):
        def next_of(z):
            old = p[z]
            y[z] = a * old
            left = q[z] - a * e[z]
            q[z] = left
            new = left + beta * old
            p[z] = new
            return new, left

        return next_of

    def later(a, beta):
        def next_of(z):
            old = p[z]
            y[z] = y[z] + a * old
            left = q[z] - a * e[z]
            q[z] = left
            new = left + beta * old
            p[z] = new
            return new, left

        return next_of

    carry = sweep(begin, cz, cx, cy)
    cz, cx, cy = full(cz), full(cx), full(cy)
    carry = sweep(second(*carry), cz, cx, cy)
    carry = lax.fori_loop(0, INNER - 2, lambda _, c: sweep(later(*c), cz, cx, cy), carry)
    a = carry[0]
    for z in range(CZ):
        local[z] = s[z] * (y[z] + a * p[z])


def solve0_body(ins, outs, p, q, e, y, ky):
    flags, *halos, k, storage, r = ins
    local, s, sinv, cz, cx, cy, bounds_zx, bounds_y = outs
    sub, lane = iota((CX, CY), 0), iota((CX, CY), 1)
    zl, zh, xl, xh, y_rows = halo_values(flags, halos)
    zl, zh, xl, xh = flags[0] * zl, flags[1] * zh, flags[2] * xl, flags[3] * xh
    y_flags = jnp.where(iota((8, LINES), 0) == 0, flags[4], flags[5])
    y_rows = y_flags * y_rows
    ky[...] = edge_field(y_rows)
    zx, by = raw(bounds_zx), raw(bounds_y)
    zx[0:32, :] = flags[0] * 0.5 * (k[0] + zl)
    planes = []
    for z in range(CZ):
        c = k[z]
        planes.append(c.astype(BF16))
        x_row_lo, x_row_hi = xl[z : z + 1, :], xh[z : z + 1, :]
        zx[64 + z : 65 + z, :] = flags[2] * 0.5 * (c[0:1, :] + x_row_lo)
        zx[80 + z : 81 + z, :] = flags[3] * 0.5 * (c[CX - 1 : CX, :] + x_row_hi)
        around = (k[z - 1] if z else zl) + (k[z + 1] if z + 1 < CZ else zh)
        right = pltpu.roll(c, CX - 1, 0)
        around = around + jnp.where(sub == CX - 1, x_row_hi, right)
        around = around + jnp.where(sub == 0, x_row_lo, pltpu.roll(c, 1, 0))
        ahead = pltpu.roll(c, CY - 1, 1)
        beyond = ky[z * CX : (z + 1) * CX, :]
        around = around + jnp.where(lane == CY - 1, beyond, ahead)
        around = around + jnp.where(lane == 0, beyond, pltpu.roll(c, 1, 1))
        diagonal = storage[z] + 3.0 * c + 0.5 * around
        root = lax.rsqrt(diagonal)
        root = root * (1.5 - 0.5 * diagonal * root * root)
        s[z] = root
        sinv[z] = diagonal * root
        cx[z] = jnp.where(sub == CX - 1, 0.0, 0.5 * (c + right) * root * pltpu.roll(root, CX - 1, 0))
        cy[z] = jnp.where(lane == CY - 1, 0.0, 0.5 * (c + ahead) * root * pltpu.roll(root, CY - 1, 1))
        if z:
            cz[z - 1] = 0.5 * (k[z - 1] + c) * s[z - 1] * root
    cz[CZ - 1] = jnp.zeros((CX, CY), F32)
    zx[32:64, :] = flags[1] * 0.5 * (k[CZ - 1] + zh)
    by[...] = y_flags * 0.5 * (edge_rows(jnp.concatenate(planes, axis=0)) + y_rows)
    bounds_zx.send()
    bounds_y.send()
    cg(raw(cz), raw(cx), raw(cy), raw(s), p, q, e, y, lambda z: s[z] * r[z], local)


def solve1_body(ins, outs, p, q, e, y):
    scalars, r, image, s, cz, cx, cy = ins
    (local,) = outs
    alpha = full(scalars)[0:1, 0:1]
    cg(cz, cx, cy, s, p, q, e, y, lambda z: s[z] * (r[z] - alpha * image[z]), local)


def combine_body(ins, outs, xs_lo, xs_hi, wide, lines, sems):
    flags, got, hits, take, factor, local, *_ = ins
    out, kept, *faces = outs
    wide[...] = got[...].astype(F32)
    factor = full(factor)
    flipped = wide[part_rows(EXTRA), :].T
    u = flipped[0:32, :] + flipped[32:64, :]
    acc = jnp.zeros((KC, LANES), F32)
    for t in range(32):
        acc = acc + factor[:, t * LANES : (t + 1) * LANES] * u[t : t + 1, :]
    coef_col = jnp.sum(acc, axis=1, keepdims=True)
    pieces = split3(jnp.broadcast_to(coef_col, (KC, CY)))
    coef = jnp.concatenate([*pieces, jnp.zeros((LANES - 3 * KC, CY), F32)], axis=0)
    lines[...] = jnp.dot(full(hits)[...], coef.astype(BF16), preferred_element_type=F32)
    back = jnp.concatenate(
        [
            jnp.concatenate([wide[part_rows(k), :], wide[part_rows(CAP + k), :]], axis=1)
            for k in range(CAP)
        ],
        axis=0,
    ).astype(BF16)
    placed = jnp.dot(full(take)[...], back, preferred_element_type=F32)
    order = {0: 0, 1: 1, CZ - 2: 2, CZ - 1: 3}
    for z in range(CZ):
        plane = local[z] + lines[z * CX : (z + 1) * CX, :]
        if z in order:
            at = order[z] * CX
            plane = plane + placed[at : at + CX, :]
        out[z] = plane
    keep = pltpu.make_async_copy(out, kept, sems)
    keep.start()
    face_store(lambda z: out[z], flags, faces, xs_lo, xs_hi)
    keep.wait()


def apply_layers(v, sinv, cz, cx, cy, zx, by, flags, halos, beyond):
    zl, zh, xl, xh, y_rows = halo_values(flags, halos)
    beyond[...] = edge_field(by[...] * y_rows)
    xl, xh = zx[64:80, :] * xl, zx[80:96, :] * xh
    sub = iota((CX, CY), 0)
    first_row, last_row = sub == 0, sub == CX - 1
    below, now = None, v[0] * sinv[0]
    for z in range(CZ):
        above = v[z + 1] * sinv[z + 1] if z + 1 < CZ else None
        scaled = minus_neighbours(
            now,
            below,
            above,
            cz[z - 1] if z else None,
            cz[z] if z + 1 < CZ else None,
            cx[z],
            cy[z],
        )
        out = scaled * sinv[z] - beyond[z * CX : (z + 1) * CX, :]
        row = jnp.where(first_row, xl[z : z + 1, :], 0.0)
        out = out - jnp.where(last_row, xh[z : z + 1, :], row)
        if z == 0:
            out = out - zx[0:32, :] * zl
        if z == CZ - 1:
            out = out - zx[32:64, :] * zh
        yield z, out
        below, now = now, above


def apply0_body(ins, outs, tile, rows, wide, beyond):
    flags, v, sinv, cz, cx, cy, zx, by, r, *halos, hits, put, factor = ins
    image, send = outs
    rz = jnp.zeros((8, LANES), F32)
    curvature = jnp.zeros((8, LANES), F32)
    lines = []
    for z, out in apply_layers(v, sinv, cz, cx, cy, zx, by, flags, halos, beyond):
        image[z] = out
        lines.append(jnp.sum(out, axis=1, keepdims=True))
        rz = rz + fold(r[z] * v[z])
        curvature = curvature + fold(v[z] * out)
    u_rows = coarse_rows(lambda z: lines[z], full(hits), factor, rows)
    sums = (total(rz), total(curvature))
    store_send(raw(send), face_blocks(image), full(put)[...], u_rows, sums, tile, wide)


def apply1_body(ins, outs, beyond):
    flags, v, sinv, cz, cx, cy, zx, by, r, image0, *halos, scalars = ins
    image, sums = outs
    alpha = full(scalars)[0:1, 0:1]
    sums3 = [jnp.zeros((8, LANES), F32) for _ in range(3)]
    for z, out in apply_layers(v, sinv, cz, cx, cy, zx, by, flags, halos, beyond):
        image[z] = out
        at = v[z]
        sums3[0] = sums3[0] + fold((r[z] - alpha * image0[z]) * at)
        sums3[1] = sums3[1] + fold(at * out)
        sums3[2] = sums3[2] + fold(at * image0[z])
    lane = iota((ZN, LANES), 1)
    row = jnp.zeros((ZN, LANES), F32)
    for i in range(3):
        row = jnp.where(lane == i, total(sums3[i]), row)
    sums[...] = row


def final_body(ins, outs):
    scalars, got, d, v, r, image0, image1 = ins
    solution, residual = outs
    scalars = full(scalars)
    sums = jnp.sum(got[...], axis=0, keepdims=True)
    alpha0, rz0, curvature0 = scalars[0:1, 0:1], scalars[1:2, 0:1], scalars[2:3, 0:1]
    rz1, vav, vad = sums[:, 0:1], sums[:, 1:2], sums[:, 2:3]
    beta = rz1 / rz0
    alpha1 = rz1 / (vav + 2.0 * beta * vad + beta * beta * curvature0)
    mix = alpha0 + alpha1 * beta
    for z in range(CZ):
        solution[z] = mix * d[z] + alpha1 * v[z]
        residual[z] = r[z] - mix * image0[z] - alpha1 * image1[z]


FIELD = sds((CZ, CX, CY))
FIELD_SCRATCH = pltpu.VMEM((CZ, CX, CY), F32)
PACKED = sds((ZN * PARTS, LANES), BF16)
WIDE = pltpu.VMEM((ZN * PARTS, LANES), F32)
TILE = pltpu.VMEM((LANES, LANES), F32)
ROWS = pltpu.VMEM((KC, LANES), F32)
LINE_FIELD = pltpu.VMEM((LINES, CY), F32)
HITS = sds((LINES, LANES), BF16)
PUT = sds((CAP * ZN, ZN), BF16)
TAKE = sds((ZN, CAP * ZN), BF16)


def swap(x):
    return lax.all_to_all(x, AX, split_axis=0, concat_axis=0, tiled=True)


def swap_packed(x):
    return swap(x.reshape(ZN, PARTS // 2, 2, LANES)).reshape(ZN * PARTS, LANES)


def each(mode, *arrays):
    return [(mode, a) for a in arrays]


def per_device(r, storage, k, label, zone_of_block, factor, zone_factor):
    zrow = zone_of_block.reshape(1, ZN)
    label = label.reshape(CZ, CX)
    flags = jnp.stack(
        [
            (lax.axis_index(axis) != edge).astype(F32)
            for axis in ("gz", "gx", "gy")
            for edge in (0, lax.axis_size(axis) - 1)
        ]
        + [(1 - lax.axis_index(axis) % 2).astype(F32) for axis in ("gz", "gx", "gy")]
    )
    send0, hits, put, take, *k_faces = run(
        pack_body,
        each("s", flags) + each("h", label, zrow) + each("c", r) + each("h", factor) + each("c", k),
        each("h", PACKED, HITS, PUT, TAKE, *FACE_OUTS),
        (TILE, ROWS, WIDE) + FACE_SCRATCH,
    )
    got0 = swap_packed(send0)
    k_halos = exchange(k_faces)
    got0, *k_halos = lax.optimization_barrier((got0, *k_halos))
    back0, got0 = run(
        lift0_body,
        each("v", got0) + each("h", zone_factor),
        each("c", PACKED) + each("o", PACKED),
        (WIDE, pltpu.SemaphoreType.DMA),
    )
    back0 = swap_packed(back0)
    local, s, sinv, cz, cx, cy, *bounds = run(
        solve0_body,
        each("s", flags) + each("a", *k_halos) + each("c", k, storage, r),
        each("c", *(FIELD,) * 6) + each("h", sds((96, CY)), sds((8, LINES))),
        (FIELD_SCRATCH,) * 4 + (LINE_FIELD,),
        ((7, 8, 9),),
    )
    matrix = (sinv, cz, cx, cy, *bounds)

    def combine(local, back, more):
        field, kept, *rest = run(
            combine_body,
            each("s", flags)
            + each("v", back)
            + each("h", hits, take, factor)
            + each("c", local)
            + each("p", *matrix, *more),
            each("v", FIELD) + each("o", FIELD) + each("v", *FACE_OUTS),
            FACE_SCRATCH + (WIDE, LINE_FIELD, pltpu.SemaphoreType.DMA),
        )
        return field, kept, exchange(rest[:5]), rest[5:]

    field, d, halos, passed = combine(local, back0, (r,))
    image0, send1 = run(
        apply0_body,
        each("s", flags) + each("v", field, *passed, *halos) + each("h", hits, put, factor),
        each("c", FIELD) + each("h", PACKED),
        (TILE, ROWS, WIDE, LINE_FIELD),
    )
    got1 = swap_packed(send1)
    back1, scalars = run(
        lift1_body,
        each("h", zone_factor, got0) + each("v", got1),
        each("c", PACKED) + each("h", sds((8, LANES))),
        (WIDE,),
    )
    back1 = swap_packed(back1)
    (local,) = run(
        solve1_body,
        each("h", scalars) + each("c", r, image0, s, cz, cx, cy),
        each("c", FIELD),
        (FIELD_SCRATCH,) * 4,
        ((1, 2, 3), (4, 5, 6)),
    )
    field, v, halos, passed = combine(local, back1, (r, image0))
    image1, sums = run(
        apply1_body,
        each("s", flags) + each("v", field, *passed, *halos) + each("h", scalars),
        each("c", FIELD) + each("v", sds((ZN, LANES))),
        (LINE_FIELD,),
    )
    return run(
        final_body,
        each("h", scalars) + each("v", swap(sums)) + each("c", d, v, r, image0, image1),
        each("c", FIELD, FIELD),
        (),
        ((2, 3, 4, 5, 6),),
    )


def solution(mesh):
    field = P("gz", "gx", "gy")
    in_specs = (field, field, field, field, P(AX, None), P(AX, None), P(AX, None, None))
    return jax.shard_map(
        per_device, mesh=mesh, in_specs=in_specs, out_specs=(field, field), check_vma=False
    )
```

```python
import jax
import jax.numpy as jnp
from jax import lax
from jax.experimental import pallas as pl
from jax.experimental.pallas import tpu as pltpu
from jax.sharding import PartitionSpec as P

CZ = 16
CX = 32
CY = 256
KC = 32
INNER = 8
CAP = 4
ZN = 128
FB = 256
EXTRA = 2 * CAP
PARTS = EXTRA + 2
LANES = 128
LINES = CZ * CX
AX = ("gx", "gy", "gz")
F32 = jnp.float32
BF16 = jnp.bfloat16

def sds(shape, dtype=F32):
    return jax.ShapeDtypeStruct(shape, dtype)


class Load:
    def __init__(self, source, buffer, sems, chunks):
        self.buffer = buffer
        self.size = buffer.shape[0] // chunks
        self.copies = []
        for i in range(chunks):
            part = pl.ds(i * self.size, self.size)
            self.copies.append(
                pltpu.make_async_copy(source.at[part], buffer.at[part], sems.at[i])
            )

    def start(self, i):
        self.copies[i].start()

    def wait(self, i):
        if self.copies[i] is not None:
            self.copies[i].wait()
            self.copies[i] = None

    def full(self):
        for i in range(len(self.copies)):
            self.wait(i)
        return self.buffer

    def __getitem__(self, z):
        self.wait(z // self.size)
        return self.buffer[z]


class Store:
    def __init__(self, target, buffer, sems, chunks):
        self.buffer, self.target, self.sems = buffer, target, sems
        self.size = buffer.shape[0] // chunks
        self.copies = [None] * chunks

    def flush(self, i):
        part = pl.ds(i * self.size, self.size)
        copy = pltpu.make_async_copy(self.buffer.at[part], self.target.at[part], self.sems.at[i])
        copy.start()
        self.copies[i] = copy

    def __setitem__(self, z, value):
        self.buffer[z] = value
        if z % self.size == self.size - 1:
            self.flush(z // self.size)

    def __getitem__(self, z):
        return self.buffer[z]

    def send(self):
        for i, copy in enumerate(self.copies):
            if copy is None:
                self.flush(i)

    def finish(self):
        self.send()
        for copy in self.copies:
            copy.wait()


SPACE = {"a": pl.ANY, "o": pltpu.HBM, "s": pltpu.SMEM, "v": pltpu.VMEM, "h": pltpu.HBM, "c": pltpu.HBM, "p": pltpu.HBM}
COPIED = "hcpa"
CHUNKS = 4


def chunks_of(mode, array):
    return CHUNKS if mode in "cp" and array.shape[0] > 8 else 1


def spec(mode):
    return pl.BlockSpec(memory_space=SPACE[mode])


def run(body, ins, outs, scratch=(), mixed=()):
    moved = [(m, a) for side in (ins, outs) for m, a in side if m in COPIED]
    n_chunks = [chunks_of(m, a) for m, a in moved]
    buffers = [pltpu.VMEM(a.shape, a.dtype) for m, a in moved if m != "p"]
    sems = [pltpu.SemaphoreType.DMA((n,)) for n in n_chunks]
    passed = [sds(a.shape, a.dtype) for m, a in ins if m == "p"]
    n_in, n_out, n_pass, n_own = len(ins), len(outs), len(passed), len(scratch)

    def kernel(*refs):
        refs = list(refs)

        def take(n):
            head = refs[:n]
            del refs[:n]
            return head

        in_refs, out_refs, pass_refs, own = take(n_in), take(n_out), take(n_pass), take(n_own)
        bufs = take(len(buffers))
        given, made, loads, stores = [], [], [], []
        for (m, _), ref in zip(ins, in_refs):
            if m in COPIED:
                buf = pass_refs.pop(0) if m == "p" else bufs.pop(0)
                given.append(Load(ref, buf, refs.pop(0), chunks_of(m, buf)))
                loads.append(given[-1])
            else:
                given.append(ref)
        for (m, _), ref in zip(outs, out_refs):
            if m in COPIED:
                made.append(Store(ref, bufs[0], refs.pop(0), chunks_of(m, bufs.pop(0))))
                stores.append(made[-1])
            else:
                made.append(ref)
        groups = {id(given[g[0]]): [given[i] for i in g] for g in mixed}
        joined = [id(given[i]) for g in mixed for i in g]
        for x in loads:
            for i in range(len(x.copies)):
                if id(x) not in joined:
                    x.start(i)
                for one in groups.get(id(x), ()):
                    one.start(i)
        body(given, made, *own)
        for x in stores:
            x.send()
        for x in loads:
            x.full()
        for x in stores:
            x.finish()

    return pl.pallas_call(
        kernel,
        out_shape=tuple(
            pltpu.HBM(a.shape, a.dtype) if m in "hco" else a for m, a in outs
        )
        + tuple(passed),
        in_specs=[spec(m) for m, _ in ins],
        out_specs=tuple(spec(m) for m, _ in outs) + (spec("v"),) * n_pass,
        scratch_shapes=tuple(scratch) + tuple(buffers) + tuple(sems),
        compiler_params=pltpu.CompilerParams(vmem_limit_bytes=24 * 1024 * 1024),
    )(*[pltpu.with_memory_space_constraint(a, pltpu.HBM) if m in "hcp" else a for m, a in ins])


def full(x):
    return x.full() if isinstance(x, Load) else x


def raw(x):
    return x.buffer if isinstance(x, (Load, Store)) else x


def iota(shape, dim):
    return lax.broadcasted_iota(jnp.int32, shape, dim)


def total(x):
    return jnp.sum(jnp.sum(x, axis=1, keepdims=True), axis=0, keepdims=True)


def fold(x):
    half = x[:, :LANES] + x[:, LANES:]
    return half[0:8] + half[8:16] + half[16:24] + half[24:32]


def split3(x):
    high = x.astype(BF16).astype(F32)
    rest = x - high
    mid = rest.astype(BF16).astype(F32)
    return high, mid, rest - mid


def choose(even, first, second):
    return even * first + (1.0 - even) * second


def edge_rows(flat):
    shape = (8, CY)
    sub, lane = iota(shape, 0), iota(shape, 1)
    hit = ((sub == 0) & (lane == 0)) | ((sub == 1) & (lane == CY - 1))
    pick = jnp.where(hit, 1.0, 0.0).astype(BF16)
    return lax.dot_general(pick, flat, (((1,), (1,)), ((), ())), preferred_element_type=F32)


def edge_field(rows):
    high, mid, low = split3(rows)
    sub = iota(rows.shape, 0)
    stack = jnp.where(
        sub < 2, high, jnp.where(sub < 4, pltpu.roll(mid, 2, 0), pltpu.roll(low, 4, 0))
    )
    shape = (8, CY)
    sub, lane = iota(shape, 0), iota(shape, 1)
    hit = ((sub % 2 == 0) & (lane == 0)) | ((sub % 2 == 1) & (lane == CY - 1))
    put = jnp.where(hit & (sub < 6), 1.0, 0.0).astype(BF16)
    stack = jnp.where(iota(rows.shape, 0) < 6, stack, 0.0)
    return jnp.dot(stack.T.astype(BF16), put, preferred_element_type=F32)


def face_store(plane_of, flags, refs, xs_lo, xs_hi):
    za, zb, xa, xb, ys = (raw(x) for x in refs)
    low, high = plane_of(0), plane_of(CZ - 1)
    za[...] = choose(flags[6], high, low).astype(BF16)
    zb[...] = choose(flags[6], low, high).astype(BF16)
    planes = []
    for z in range(CZ):
        plane = plane_of(z)
        xs_lo[z : z + 1, :] = plane[0:1, :]
        xs_hi[z : z + 1, :] = plane[CX - 1 : CX, :]
        planes.append(plane.astype(BF16))
    xa[...] = choose(flags[7], xs_hi[...], xs_lo[...]).astype(BF16)
    xb[...] = choose(flags[7], xs_lo[...], xs_hi[...]).astype(BF16)
    ys[...] = edge_rows(jnp.concatenate(planes, axis=0)).astype(BF16)


FACE_OUTS = (
    sds((CX, CY), BF16),
    sds((CX, CY), BF16),
    sds((CZ, CY), BF16),
    sds((CZ, CY), BF16),
    sds((8, LINES), BF16),
)
FACE_SCRATCH = (pltpu.VMEM((CZ, CY), F32), pltpu.VMEM((CZ, CY), F32))


def pair(axis, first, second):
    n = lax.axis_size(axis)
    even = [(i, i ^ 1) for i in range(n)]
    odd = [(i, (i + 1 if i % 2 else i - 1) % n) for i in range(n)]
    return [lax.ppermute(first, axis, even), lax.ppermute(second, axis, odd)]


def exchange(faces):
    za, zb, xa, xb, ys = faces
    return pair("gz", za, zb) + pair("gx", xa, xb) + pair("gy", ys, ys)


def halo_values(flags, got):
    za, zb, xa, xb, ya, yb = (full(x)[...].astype(F32) for x in got)
    low, high = choose(flags[8], yb, ya), choose(flags[8], ya, yb)
    shape = (8, LINES)
    sub = iota(shape, 0)
    rows = jnp.where(
        sub == 0,
        jnp.broadcast_to(low[1:2, :], shape),
        jnp.where(sub == 1, jnp.broadcast_to(high[0:1, :], shape), 0.0),
    )
    return (
        choose(flags[6], zb, za),
        choose(flags[6], za, zb),
        choose(flags[7], xb, xa),
        choose(flags[7], xa, xb),
        rows,
    )


def slots(zrow):
    shape = (ZN, ZN)
    sub, lane = iota(shape, 0), iota(shape, 1)
    row = jnp.broadcast_to(zrow, shape)
    zcol = jnp.sum(jnp.where(sub == lane, row, 0), axis=1, keepdims=True)
    same = row == zcol
    slot_row = jnp.sum(jnp.where(same & (sub < lane), 1, 0), axis=0, keepdims=True)
    slot_col = jnp.sum(jnp.where(same & (lane < sub), 1, 0), axis=1, keepdims=True)
    return zrow + ZN * slot_row, zcol + ZN * slot_col


def part_rows(part, first=0, count=ZN):
    return pl.ds(first * PARTS + part, count, stride=PARTS)


def zone_hits(zrow):
    row, col = slots(zrow)
    put = jnp.where(iota((CAP * ZN, ZN), 0) == row, 1.0, 0.0).astype(BF16)
    take = jnp.where(iota((ZN, CAP * ZN), 1) == col, 1.0, 0.0).astype(BF16)
    return put, take


def store_send(send, blocks, put, u_rows, scalars, tile, wide):
    placed = jnp.dot(put, blocks, preferred_element_type=F32)
    for k in range(CAP):
        rows = placed[k * ZN : (k + 1) * ZN, :]
        wide[part_rows(k), :] = rows[:, :LANES]
        wide[part_rows(CAP + k), :] = rows[:, LANES:]
    high = u_rows.astype(BF16).astype(F32)
    tile[0:32, :] = high
    tile[32:64, :] = u_rows - high
    tile[64:128, :] = jnp.zeros((64, LANES), F32)
    for i, value in enumerate(scalars):
        for j, piece in enumerate(split3(value)):
            at = 64 + 3 * i + j
            tile[at : at + 1, :] = jnp.broadcast_to(piece, (1, LANES))
    wide[part_rows(EXTRA), :] = tile[...].T
    wide[part_rows(EXTRA + 1), :] = jnp.zeros((ZN, LANES), F32)
    send[...] = wide[...].astype(BF16)


def label_hits(label, tile, hits, flipped):
    tile[...] = jnp.zeros((LANES, LANES), F32)
    tile[0:CZ, 0:CX] = full(label)[...].astype(F32)
    columns = tile[...].T[0:CX, :]
    lane = iota((CX, LANES), 1)
    kind = jnp.where(lane < 3 * KC, lane % KC, -1).astype(F32)
    columns_of = []
    for z in range(CZ):
        hit = jnp.where(columns[:, z : z + 1] == kind, 1.0, 0.0)
        hits[z * CX : (z + 1) * CX, :] = hit.astype(BF16)
        columns_of.append(hit)
    flipped[...] = jnp.concatenate(columns_of, axis=0).T[0:KC, :].astype(BF16)


def store_split(plane, z, high, low):
    top = plane.astype(BF16)
    high[z * CX : (z + 1) * CX, :] = top
    low[z * CX : (z + 1) * CX, :] = (plane - top.astype(F32)).astype(BF16)


def coarse_rows(high, low, flipped, factor, rows):
    hits = flipped[0:KC, :]
    sums = jnp.dot(hits, high[...], preferred_element_type=F32)
    sums = sums + jnp.dot(hits, low[...], preferred_element_type=F32)
    g_col = jnp.sum(sums[:, :LANES] + sums[:, LANES:], axis=1, keepdims=True)
    g = jnp.broadcast_to(g_col, (KC, LANES))
    factor = full(factor)
    for t in range(32):
        rows[t : t + 1, :] = jnp.sum(
            factor[:, t * LANES : (t + 1) * LANES] * g, axis=0, keepdims=True
        )
    return rows[...]


def face_blocks(field):
    return jnp.concatenate([field[0], field[1], field[CZ - 2], field[CZ - 1]], axis=0).astype(BF16)


def pack_body(ins, outs, tile, rows, wide, xs_lo, xs_hi, fhigh, flow):
    flags, label, zrow, r, factor, k = ins
    send, hits, flipped, put, take, *faces = outs
    label_hits(label, tile, raw(hits), raw(flipped))
    raw(put)[...], raw(take)[...] = zone_hits(full(zrow)[...])
    for x in (hits, flipped, put, take):
        x.send()
    for z in range(CZ):
        store_split(r[z], z, fhigh, flow)
    u_rows = coarse_rows(fhigh, flow, raw(flipped), factor, rows)
    store_send(raw(send), face_blocks(r), raw(put)[...], u_rows, (), tile, wide)
    send.send()
    face_store(lambda z: k[z], flags, faces, xs_lo, xs_hi)


def lift_store(out, wide, tail, zone):
    factor = zone[0]
    lane = iota((1, LANES), 1)
    u = jnp.where(lane < 32, tail + pltpu.roll(tail, LANES - 32, 1), 0.0)
    high = u.astype(BF16).astype(F32)
    both = high + pltpu.roll(u - high, 32, 1)
    size = ZN // CHUNKS
    for i in range(CHUNKS):
        at = i * size
        x = jnp.concatenate(
            [
                jnp.concatenate(
                    [wide[part_rows(k, at, size), :], wide[part_rows(CAP + k, at, size), :]],
                    axis=1,
                )
                for k in range(CAP)
            ],
            axis=0,
        ).astype(BF16)
        lifted = jnp.dot(x, factor, preferred_element_type=F32).astype(BF16)
        back = lax.dot_general(
            lifted, factor, (((1,), (1,)), ((), ())), preferred_element_type=F32
        )
        for k in range(CAP):
            rows = back[k * size : (k + 1) * size, :]
            wide[part_rows(k, at, size), :] = rows[:, :LANES]
            wide[part_rows(CAP + k, at, size), :] = rows[:, LANES:]
        wide[part_rows(EXTRA, at, size), :] = jnp.broadcast_to(both, (size, LANES))
        part = slice(at * PARTS, (at + size) * PARTS)
        out.buffer[part, :] = wide[part, :].astype(BF16)
        out.flush(i)


def tail_sum(wide):
    return jnp.sum(wide[part_rows(EXTRA), :], axis=0, keepdims=True)


def lift0_body(ins, outs, wide, sem):
    got, zone = ins
    out, kept = outs
    keep = pltpu.make_async_copy(got, kept, sem)
    keep.start()
    wide[...] = got[...].astype(F32)
    lift_store(out, wide, tail_sum(wide), full(zone))
    keep.wait()


def lift1_body(ins, outs, wide):
    zone, got0, got1 = ins
    out, scalars = outs
    store, scalars = scalars, raw(scalars)
    wide[...] = got1[...].astype(F32)
    tail1 = tail_sum(wide)
    lane = iota((1, LANES), 1)

    def scalar(i):
        keep = (lane >= 64 + 3 * i) & (lane < 67 + 3 * i)
        return jnp.sum(jnp.where(keep, tail1, 0.0), axis=1, keepdims=True)

    rz, curvature = scalar(0), scalar(1)
    alpha = rz / curvature
    scalars[0:1, :] = jnp.broadcast_to(alpha, (1, LANES))
    scalars[1:2, :] = jnp.broadcast_to(rz, (1, LANES))
    scalars[2:3, :] = jnp.broadcast_to(curvature, (1, LANES))
    scalars[3:8, :] = jnp.zeros((5, LANES), F32)
    store.send()
    wide[...] = full(got0)[...].astype(F32) - alpha * wide[...]
    lift_store(out, wide, tail_sum(wide), full(zone))


def minus_neighbours(p, below, above, cz_below, cz_above, cx, cy):
    tx = cx * p
    ty = cy * p
    out = p - cx * pltpu.roll(p, CX - 1, 0) - pltpu.roll(tx, 1, 0)
    out = out - cy * pltpu.roll(p, CY - 1, 1) - pltpu.roll(ty, 1, 1)
    if below is not None:
        out = out - cz_below * below
    if above is not None:
        out = out - cz_above * above
    return out


def cg(cz, cx, cy, s, p, q, e, y, first, local):
    def sweep(next_of, cz, cx, cy):
        rho = jnp.zeros((8, LANES), F32)
        pe, ee = rho, rho
        below, (now, left) = None, next_of(0)
        for z in range(CZ):
            rho = rho + fold(left * left)
            above = None
            if z + 1 < CZ:
                above, left = next_of(z + 1)
            image = minus_neighbours(
                now,
                below,
                above,
                cz[z - 1] if z else None,
                cz[z] if z + 1 < CZ else None,
                cx[z],
                cy[z],
            )
            e[z] = image
            pe = pe + fold(now * image)
            ee = ee + fold(image * image)
            below, now = now, above
        rho, pe, ee = total(rho), total(pe), total(ee)
        a = rho / pe
        return a, a * a * ee / rho - 1.0

    def begin(z):
        value = first(z)
        q[z] = value
        p[z] = value
        return value, value

    def second(a, beta):
        def next_of(z):
            old = p[z]
            y[z] = a * old
            left = q[z] - a * e[z]
            q[z] = left
            new = left + beta * old
            p[z] = new
            return new, left

        return next_of

    def later(a, beta):
        def next_of(z):
            old = p[z]
            y[z] = y[z] + a * old
            left = q[z] - a * e[z]
            q[z] = left
            new = left + beta * old
            p[z] = new
            return new, left

        return next_of

    carry = sweep(begin, cz, cx, cy)
    cz, cx, cy = full(cz), full(cx), full(cy)
    carry = sweep(second(*carry), cz, cx, cy)
    carry = lax.fori_loop(0, INNER - 2, lambda _, c: sweep(later(*c), cz, cx, cy), carry)
    a = carry[0]
    for z in range(CZ):
        local[z] = s[z] * (y[z] + a * p[z])


def solve0_body(ins, outs, p, q, e, y, ky):
    flags, *halos, k, storage, r = ins
    local, s, sinv, cz, cx, cy, bounds_zx, bounds_y = outs
    sub, lane = iota((CX, CY), 0), iota((CX, CY), 1)
    zl, zh, xl, xh, y_rows = halo_values(flags, halos)
    zl, zh, xl, xh = flags[0] * zl, flags[1] * zh, flags[2] * xl, flags[3] * xh
    y_flags = jnp.where(iota((8, LINES), 0) == 0, flags[4], flags[5])
    y_rows = y_flags * y_rows
    ky[...] = edge_field(y_rows)
    zx, by = raw(bounds_zx), raw(bounds_y)
    zx[0:32, :] = flags[0] * 0.5 * (k[0] + zl)
    planes = []
    for z in range(CZ):
        c = k[z]
        planes.append(c.astype(BF16))
        x_row_lo, x_row_hi = xl[z : z + 1, :], xh[z : z + 1, :]
        zx[64 + z : 65 + z, :] = flags[2] * 0.5 * (c[0:1, :] + x_row_lo)
        zx[80 + z : 81 + z, :] = flags[3] * 0.5 * (c[CX - 1 : CX, :] + x_row_hi)
        around = (k[z - 1] if z else zl) + (k[z + 1] if z + 1 < CZ else zh)
        right = pltpu.roll(c, CX - 1, 0)
        around = around + jnp.where(sub == CX - 1, x_row_hi, right)
        around = around + jnp.where(sub == 0, x_row_lo, pltpu.roll(c, 1, 0))
        ahead = pltpu.roll(c, CY - 1, 1)
        beyond = ky[z * CX : (z + 1) * CX, :]
        around = around + jnp.where(lane == CY - 1, beyond, ahead)
        around = around + jnp.where(lane == 0, beyond, pltpu.roll(c, 1, 1))
        diagonal = storage[z] + 3.0 * c + 0.5 * around
        root = lax.rsqrt(diagonal)
        root = root * (1.5 - 0.5 * diagonal * root * root)
        s[z] = root
        sinv[z] = diagonal * root
        cx[z] = jnp.where(sub == CX - 1, 0.0, 0.5 * (c + right) * root * pltpu.roll(root, CX - 1, 0))
        cy[z] = jnp.where(lane == CY - 1, 0.0, 0.5 * (c + ahead) * root * pltpu.roll(root, CY - 1, 1))
        if z:
            cz[z - 1] = 0.5 * (k[z - 1] + c) * s[z - 1] * root
    cz[CZ - 1] = jnp.zeros((CX, CY), F32)
    zx[32:64, :] = flags[1] * 0.5 * (k[CZ - 1] + zh)
    by[...] = y_flags * 0.5 * (edge_rows(jnp.concatenate(planes, axis=0)) + y_rows)
    bounds_zx.send()
    bounds_y.send()
    cg(raw(cz), raw(cx), raw(cy), raw(s), p, q, e, y, lambda z: s[z] * r[z], local)


def solve1_body(ins, outs, p, q, e, y):
    scalars, r, image, s, cz, cx, cy = ins
    (local,) = outs
    alpha = full(scalars)[0:1, 0:1]
    cg(cz, cx, cy, s, p, q, e, y, lambda z: s[z] * (r[z] - alpha * image[z]), local)


def combine_body(ins, outs, xs_lo, xs_hi, wide, lines):
    flags, got, hits, take, factor, local, *_ = ins
    out, *faces = outs
    wide[...] = got[...].astype(F32)
    factor = full(factor)
    flipped = wide[part_rows(EXTRA), :].T
    u = flipped[0:32, :] + flipped[32:64, :]
    acc = jnp.zeros((KC, LANES), F32)
    for t in range(32):
        acc = acc + factor[:, t * LANES : (t + 1) * LANES] * u[t : t + 1, :]
    coef_col = jnp.sum(acc, axis=1, keepdims=True)
    pieces = split3(jnp.broadcast_to(coef_col, (KC, CY)))
    coef = jnp.concatenate([*pieces, jnp.zeros((LANES - 3 * KC, CY), F32)], axis=0)
    lines[...] = jnp.dot(full(hits)[...], coef.astype(BF16), preferred_element_type=F32)
    back = jnp.concatenate(
        [
            jnp.concatenate([wide[part_rows(k), :], wide[part_rows(CAP + k), :]], axis=1)
            for k in range(CAP)
        ],
        axis=0,
    ).astype(BF16)
    placed = jnp.dot(full(take)[...], back, preferred_element_type=F32)
    order = {0: 0, 1: 1, CZ - 2: 2, CZ - 1: 3}
    for z in range(CZ):
        plane = local[z] + lines[z * CX : (z + 1) * CX, :]
        if z in order:
            at = order[z] * CX
            plane = plane + placed[at : at + CX, :]
        out[z] = plane
    face_store(lambda z: out[z], flags, faces, xs_lo, xs_hi)


def apply_layers(v, sinv, cz, cx, cy, zx, by, flags, halos, beyond):
    zl, zh, xl, xh, y_rows = halo_values(flags, halos)
    beyond[...] = edge_field(by[...] * y_rows)
    xl, xh = zx[64:80, :] * xl, zx[80:96, :] * xh
    sub = iota((CX, CY), 0)
    first_row, last_row = sub == 0, sub == CX - 1
    below, now = None, v[0] * sinv[0]
    for z in range(CZ):
        above = v[z + 1] * sinv[z + 1] if z + 1 < CZ else None
        scaled = minus_neighbours(
            now,
            below,
            above,
            cz[z - 1] if z else None,
            cz[z] if z + 1 < CZ else None,
            cx[z],
            cy[z],
        )
        out = scaled * sinv[z] - beyond[z * CX : (z + 1) * CX, :]
        row = jnp.where(first_row, xl[z : z + 1, :], 0.0)
        out = out - jnp.where(last_row, xh[z : z + 1, :], row)
        if z == 0:
            out = out - zx[0:32, :] * zl
        if z == CZ - 1:
            out = out - zx[32:64, :] * zh
        yield z, out
        below, now = now, above


def apply0_body(ins, outs, tile, rows, wide, beyond, fhigh, flow, sem):
    flags, v, sinv, cz, cx, cy, zx, by, r, *halos, flipped, put, factor = ins
    image, send, kept = outs
    keep = pltpu.make_async_copy(v, kept, sem)
    keep.start()
    rz = jnp.zeros((8, LANES), F32)
    curvature = jnp.zeros((8, LANES), F32)
    for z, out in apply_layers(v, sinv, cz, cx, cy, zx, by, flags, halos, beyond):
        image[z] = out
        store_split(out, z, fhigh, flow)
        rz = rz + fold(r[z] * v[z])
        curvature = curvature + fold(v[z] * out)
    u_rows = coarse_rows(fhigh, flow, full(flipped), factor, rows)
    sums = (total(rz), total(curvature))
    store_send(raw(send), face_blocks(image), full(put)[...], u_rows, sums, tile, wide)
    send.send()
    keep.wait()


def apply1_body(ins, outs, beyond, sem):
    flags, v, sinv, cz, cx, cy, zx, by, r, image0, *halos = ins
    image, sums, kept = outs
    keep = pltpu.make_async_copy(v, kept, sem)
    keep.start()
    sums3 = [jnp.zeros((8, LANES), F32) for _ in range(3)]
    for z, out in apply_layers(v, sinv, cz, cx, cy, zx, by, flags, halos, beyond):
        image[z] = out
        at = v[z]
        sums3[0] = sums3[0] + fold(r[z] * at)
        sums3[1] = sums3[1] + fold(at * out)
        sums3[2] = sums3[2] + fold(at * image0[z])
    lane = iota((ZN, LANES), 1)
    row = jnp.zeros((ZN, LANES), F32)
    for i in range(3):
        row = jnp.where(lane == i, total(sums3[i]), row)
    sums[...] = row
    keep.wait()


def final_body(ins, outs):
    scalars, got, d, v, r, image0, image1 = ins
    solution, residual = outs
    scalars = full(scalars)
    sums = jnp.sum(got[...], axis=0, keepdims=True)
    alpha0, rz0, curvature0 = scalars[0:1, 0:1], scalars[1:2, 0:1], scalars[2:3, 0:1]
    rv, vav, vad = sums[:, 0:1], sums[:, 1:2], sums[:, 2:3]
    rz1 = rv - alpha0 * vad
    beta = rz1 / rz0
    alpha1 = rz1 / (vav + 2.0 * beta * vad + beta * beta * curvature0)
    mix = alpha0 + alpha1 * beta
    for z in range(CZ):
        solution[z] = mix * d[z] + alpha1 * v[z]
        residual[z] = r[z] - mix * image0[z] - alpha1 * image1[z]


FIELD = sds((CZ, CX, CY))
FIELD_SCRATCH = pltpu.VMEM((CZ, CX, CY), F32)
PACKED = sds((ZN * PARTS, LANES), BF16)
WIDE = pltpu.VMEM((ZN * PARTS, LANES), F32)
TILE = pltpu.VMEM((LANES, LANES), F32)
ROWS = pltpu.VMEM((KC, LANES), F32)
LINE_FIELD = pltpu.VMEM((LINES, CY), F32)
HITS = sds((LINES, LANES), BF16)
FLIPPED = sds((KC, LINES), BF16)
FLAT = pltpu.VMEM((LINES, CY), BF16)
PUT = sds((CAP * ZN, ZN), BF16)
TAKE = sds((ZN, CAP * ZN), BF16)


def swap(x):
    return lax.all_to_all(x, AX, split_axis=0, concat_axis=0, tiled=True)


def swap_packed(x):
    return swap(x.reshape(ZN, PARTS // 2, 2, LANES)).reshape(ZN * PARTS, LANES)


def each(mode, *arrays):
    return [(mode, a) for a in arrays]


def per_device(r, storage, k, label, zone_of_block, factor, zone_factor):
    zrow = zone_of_block.reshape(1, ZN)
    label = label.reshape(CZ, CX)
    flags = jnp.stack(
        [
            (lax.axis_index(axis) != edge).astype(F32)
            for axis in ("gz", "gx", "gy")
            for edge in (0, lax.axis_size(axis) - 1)
        ]
        + [(1 - lax.axis_index(axis) % 2).astype(F32) for axis in ("gz", "gx", "gy")]
    )
    send0, hits, flipped, put, take, *k_faces = run(
        pack_body,
        each("s", flags) + each("h", label, zrow) + each("c", r) + each("h", factor) + each("c", k),
        each("h", PACKED, HITS, FLIPPED, PUT, TAKE, *FACE_OUTS),
        (TILE, ROWS, WIDE) + FACE_SCRATCH + (FLAT, FLAT),
    )
    got0 = swap_packed(send0)
    k_halos = exchange(k_faces)
    got0, *k_halos = lax.optimization_barrier((got0, *k_halos))
    back0, got0 = run(
        lift0_body,
        each("v", got0) + each("h", zone_factor),
        each("c", PACKED) + each("o", PACKED),
        (WIDE, pltpu.SemaphoreType.DMA),
    )
    back0 = swap_packed(back0)
    local, s, sinv, cz, cx, cy, *bounds = run(
        solve0_body,
        each("s", flags) + each("a", *k_halos) + each("c", k, storage, r),
        each("c", *(FIELD,) * 6) + each("h", sds((96, CY)), sds((8, LINES))),
        (FIELD_SCRATCH,) * 4 + (LINE_FIELD,),
        ((7, 8, 9),),
    )
    matrix = (sinv, cz, cx, cy, *bounds)

    def combine(local, back, more):
        field, *rest = run(
            combine_body,
            each("s", flags)
            + each("v", back)
            + each("h", hits, take, factor)
            + each("c", local)
            + each("p", *matrix, *more),
            each("v", FIELD, *FACE_OUTS),
            FACE_SCRATCH + (WIDE, LINE_FIELD),
        )
        return field, exchange(rest[:5]), rest[5:]

    field, halos, passed = combine(local, back0, (r,))
    image0, send1, d = run(
        apply0_body,
        each("s", flags) + each("v", field, *passed, *halos) + each("h", flipped, put, factor),
        each("c", FIELD) + each("h", PACKED) + each("o", FIELD),
        (TILE, ROWS, WIDE, LINE_FIELD, FLAT, FLAT, pltpu.SemaphoreType.DMA),
    )
    got1 = swap_packed(send1)
    back1, scalars = run(
        lift1_body,
        each("h", zone_factor, got0) + each("v", got1),
        each("c", PACKED) + each("h", sds((8, LANES))),
        (WIDE,),
    )
    back1 = swap_packed(back1)
    (local,) = run(
        solve1_body,
        each("h", scalars) + each("c", r, image0, s, cz, cx, cy),
        each("c", FIELD),
        (FIELD_SCRATCH,) * 4,
        ((1, 2, 3), (4, 5, 6)),
    )
    field, halos, passed = combine(local, back1, (r, image0))
    image1, sums, v = run(
        apply1_body,
        each("s", flags) + each("v", field, *passed, *halos),
        each("c", FIELD) + each("v", sds((ZN, LANES))) + each("o", FIELD),
        (LINE_FIELD, pltpu.SemaphoreType.DMA),
    )
    return run(
        final_body,
        each("h", scalars) + each("v", swap(sums)) + each("c", d, v, r, image0, image1),
        each("c", FIELD, FIELD),
        (),
        ((2, 3, 4, 5, 6),),
    )


def solution(mesh):
    field = P("gz", "gx", "gy")
    in_specs = (field, field, field, field, P(AX, None), P(AX, None), P(AX, None, None))
    return jax.shard_map(
        per_device, mesh=mesh, in_specs=in_specs, out_specs=(field, field), check_vma=False
    )
```

```python
import jax
import jax.numpy as jnp
from jax import lax
from jax.experimental import pallas as pl
from jax.experimental.pallas import tpu as pltpu
from jax.sharding import PartitionSpec as P

CZ = 16
CX = 32
CY = 256
KC = 32
INNER = 8
CAP = 4
ZN = 128
FB = 256
EXTRA = 2 * CAP
PARTS = EXTRA + 2
LANES = 128
LINES = CZ * CX
AX = ("gx", "gy", "gz")
F32 = jnp.float32
BF16 = jnp.bfloat16

def sds(shape, dtype=F32):
    return jax.ShapeDtypeStruct(shape, dtype)


class Load:
    def __init__(self, source, buffer, sems, chunks):
        self.buffer = buffer
        self.size = buffer.shape[0] // chunks
        self.copies = []
        for i in range(chunks):
            part = pl.ds(i * self.size, self.size)
            self.copies.append(
                pltpu.make_async_copy(source.at[part], buffer.at[part], sems.at[i])
            )

    def start(self, i):
        self.copies[i].start()

    def wait(self, i):
        if self.copies[i] is not None:
            self.copies[i].wait()
            self.copies[i] = None

    def full(self):
        for i in range(len(self.copies)):
            self.wait(i)
        return self.buffer

    def __getitem__(self, z):
        self.wait(z // self.size)
        return self.buffer[z]


class Store:
    def __init__(self, target, buffer, sems, chunks):
        self.buffer, self.target, self.sems = buffer, target, sems
        self.size = buffer.shape[0] // chunks
        self.copies = [None] * chunks

    def flush(self, i):
        part = pl.ds(i * self.size, self.size)
        copy = pltpu.make_async_copy(self.buffer.at[part], self.target.at[part], self.sems.at[i])
        copy.start()
        self.copies[i] = copy

    def __setitem__(self, z, value):
        self.buffer[z] = value
        if z % self.size == self.size - 1:
            self.flush(z // self.size)

    def __getitem__(self, z):
        return self.buffer[z]

    def send(self):
        for i, copy in enumerate(self.copies):
            if copy is None:
                self.flush(i)

    def finish(self):
        self.send()
        for copy in self.copies:
            copy.wait()


SPACE = {"a": pl.ANY, "o": pltpu.HBM, "s": pltpu.SMEM, "v": pltpu.VMEM, "h": pltpu.HBM, "c": pltpu.HBM, "p": pltpu.HBM, "w": pltpu.HBM}
COPIED = "hcpaw"
CHUNKS = 2
WRITES = 2


def chunks_of(mode, array):
    return {"c": CHUNKS, "w": WRITES}.get(mode, 1)


def spec(mode):
    return pl.BlockSpec(memory_space=SPACE[mode])


def run(body, ins, outs, scratch=(), mixed=()):
    moved = [(m, a) for side in (ins, outs) for m, a in side if m in COPIED]
    n_chunks = [chunks_of(m, a) for m, a in moved]
    buffers = [pltpu.VMEM(a.shape, a.dtype) for m, a in moved if m != "p"]
    sems = [pltpu.SemaphoreType.DMA((n,)) for n in n_chunks]
    passed = [sds(a.shape, a.dtype) for m, a in ins if m == "p"]
    n_in, n_out, n_pass, n_own = len(ins), len(outs), len(passed), len(scratch)

    def kernel(*refs):
        refs = list(refs)

        def take(n):
            head = refs[:n]
            del refs[:n]
            return head

        in_refs, out_refs, pass_refs, own = take(n_in), take(n_out), take(n_pass), take(n_own)
        bufs = take(len(buffers))
        given, made, loads, stores = [], [], [], []
        for (m, _), ref in zip(ins, in_refs):
            if m in COPIED:
                buf = pass_refs.pop(0) if m == "p" else bufs.pop(0)
                given.append(Load(ref, buf, refs.pop(0), chunks_of(m, buf)))
                loads.append(given[-1])
            else:
                given.append(ref)
        for (m, _), ref in zip(outs, out_refs):
            if m in COPIED:
                made.append(Store(ref, bufs[0], refs.pop(0), chunks_of(m, bufs.pop(0))))
                stores.append(made[-1])
            else:
                made.append(ref)
        groups = {id(given[g[0]]): [given[i] for i in g] for g in mixed}
        joined = [id(given[i]) for g in mixed for i in g]
        for x in loads:
            for i in range(len(x.copies)):
                if id(x) not in joined:
                    x.start(i)
                for one in groups.get(id(x), ()):
                    one.start(i)
        body(given, made, *own)
        for x in stores:
            x.send()
        for x in loads:
            x.full()
        for x in stores:
            x.finish()

    return pl.pallas_call(
        kernel,
        out_shape=tuple(
            pltpu.HBM(a.shape, a.dtype) if m in "hcow" else a for m, a in outs
        )
        + tuple(passed),
        in_specs=[spec(m) for m, _ in ins],
        out_specs=tuple(spec(m) for m, _ in outs) + (spec("v"),) * n_pass,
        scratch_shapes=tuple(scratch) + tuple(buffers) + tuple(sems),
        compiler_params=pltpu.CompilerParams(vmem_limit_bytes=24 * 1024 * 1024),
    )(*[pltpu.with_memory_space_constraint(a, pltpu.HBM) if m in "hcp" else a for m, a in ins])


def full(x):
    return x.full() if isinstance(x, Load) else x


def raw(x):
    return x.buffer if isinstance(x, (Load, Store)) else x


def iota(shape, dim):
    return lax.broadcasted_iota(jnp.int32, shape, dim)


def total(x):
    return jnp.sum(jnp.sum(x, axis=1, keepdims=True), axis=0, keepdims=True)


def fold(x):
    half = x[:, :LANES] + x[:, LANES:]
    return half[0:8] + half[8:16] + half[16:24] + half[24:32]


def split3(x):
    high = x.astype(BF16).astype(F32)
    rest = x - high
    mid = rest.astype(BF16).astype(F32)
    return high, mid, rest - mid


def choose(even, first, second):
    return even * first + (1.0 - even) * second


def edge_rows(flat):
    shape = (8, CY)
    sub, lane = iota(shape, 0), iota(shape, 1)
    hit = ((sub == 0) & (lane == 0)) | ((sub == 1) & (lane == CY - 1))
    pick = jnp.where(hit, 1.0, 0.0).astype(BF16)
    return lax.dot_general(pick, flat, (((1,), (1,)), ((), ())), preferred_element_type=F32)


def edge_field(rows):
    high, mid, low = split3(rows)
    sub = iota(rows.shape, 0)
    stack = jnp.where(
        sub < 2, high, jnp.where(sub < 4, pltpu.roll(mid, 2, 0), pltpu.roll(low, 4, 0))
    )
    shape = (8, CY)
    sub, lane = iota(shape, 0), iota(shape, 1)
    hit = ((sub % 2 == 0) & (lane == 0)) | ((sub % 2 == 1) & (lane == CY - 1))
    put = jnp.where(hit & (sub < 6), 1.0, 0.0).astype(BF16)
    stack = jnp.where(iota(rows.shape, 0) < 6, stack, 0.0)
    return jnp.dot(stack.T.astype(BF16), put, preferred_element_type=F32)


def face_store(plane_of, flags, refs, xs_lo, xs_hi):
    za, zb, xa, xb, ys = (raw(x) for x in refs)
    low, high = plane_of(0), plane_of(CZ - 1)
    za[...] = choose(flags[6], high, low).astype(BF16)
    zb[...] = choose(flags[6], low, high).astype(BF16)
    planes = []
    for z in range(CZ):
        plane = plane_of(z)
        xs_lo[z : z + 1, :] = plane[0:1, :]
        xs_hi[z : z + 1, :] = plane[CX - 1 : CX, :]
        planes.append(plane.astype(BF16))
    xa[...] = choose(flags[7], xs_hi[...], xs_lo[...]).astype(BF16)
    xb[...] = choose(flags[7], xs_lo[...], xs_hi[...]).astype(BF16)
    ys[...] = edge_rows(jnp.concatenate(planes, axis=0)).astype(BF16)


FACE_OUTS = (
    sds((CX, CY), BF16),
    sds((CX, CY), BF16),
    sds((CZ, CY), BF16),
    sds((CZ, CY), BF16),
    sds((8, LINES), BF16),
)
FACE_SCRATCH = (pltpu.VMEM((CZ, CY), F32), pltpu.VMEM((CZ, CY), F32))


def pair(axis, first, second):
    n = lax.axis_size(axis)
    even = [(i, i ^ 1) for i in range(n)]
    odd = [(i, (i + 1 if i % 2 else i - 1) % n) for i in range(n)]
    return [lax.ppermute(first, axis, even), lax.ppermute(second, axis, odd)]


def exchange(faces):
    za, zb, xa, xb, ys = faces
    return pair("gz", za, zb) + pair("gx", xa, xb) + pair("gy", ys, ys)


def halo_values(flags, got):
    za, zb, xa, xb, ya, yb = (full(x)[...].astype(F32) for x in got)
    low, high = choose(flags[8], yb, ya), choose(flags[8], ya, yb)
    shape = (8, LINES)
    sub = iota(shape, 0)
    rows = jnp.where(
        sub == 0,
        jnp.broadcast_to(low[1:2, :], shape),
        jnp.where(sub == 1, jnp.broadcast_to(high[0:1, :], shape), 0.0),
    )
    return (
        choose(flags[6], zb, za),
        choose(flags[6], za, zb),
        choose(flags[7], xb, xa),
        choose(flags[7], xa, xb),
        rows,
    )


def slots(zrow):
    shape = (ZN, ZN)
    sub, lane = iota(shape, 0), iota(shape, 1)
    row = jnp.broadcast_to(zrow, shape)
    zcol = jnp.sum(jnp.where(sub == lane, row, 0), axis=1, keepdims=True)
    same = row == zcol
    slot_row = jnp.sum(jnp.where(same & (sub < lane), 1, 0), axis=0, keepdims=True)
    slot_col = jnp.sum(jnp.where(same & (lane < sub), 1, 0), axis=1, keepdims=True)
    return zrow + ZN * slot_row, zcol + ZN * slot_col


def part_rows(part, first=0, count=ZN):
    return pl.ds(first * PARTS + part, count, stride=PARTS)


def zone_hits(zrow):
    row, col = slots(zrow)
    put = jnp.where(iota((CAP * ZN, ZN), 0) == row, 1.0, 0.0).astype(BF16)
    take = jnp.where(iota((ZN, CAP * ZN), 1) == col, 1.0, 0.0).astype(BF16)
    return put, take


def store_send(send, blocks, put, u_rows, scalars, tile, wide):
    placed = jnp.dot(put, blocks, preferred_element_type=F32)
    for k in range(CAP):
        rows = placed[k * ZN : (k + 1) * ZN, :]
        wide[part_rows(k), :] = rows[:, :LANES]
        wide[part_rows(CAP + k), :] = rows[:, LANES:]
    high = u_rows.astype(BF16).astype(F32)
    tile[0:32, :] = high
    tile[32:64, :] = u_rows - high
    tile[64:128, :] = jnp.zeros((64, LANES), F32)
    for i, value in enumerate(scalars):
        for j, piece in enumerate(split3(value)):
            at = 64 + 3 * i + j
            tile[at : at + 1, :] = jnp.broadcast_to(piece, (1, LANES))
    wide[part_rows(EXTRA), :] = tile[...].T
    wide[part_rows(EXTRA + 1), :] = jnp.zeros((ZN, LANES), F32)
    send[...] = wide[...].astype(BF16)


def label_hits(label, tile, hits, flipped):
    tile[...] = jnp.zeros((LANES, LANES), F32)
    tile[0:CZ, 0:CX] = full(label)[...].astype(F32)
    columns = tile[...].T[0:CX, :]
    lane = iota((CX, LANES), 1)
    kind = jnp.where(lane < 3 * KC, lane % KC, -1).astype(F32)
    columns_of = []
    for z in range(CZ):
        hit = jnp.where(columns[:, z : z + 1] == kind, 1.0, 0.0)
        hits[z * CX : (z + 1) * CX, :] = hit.astype(BF16)
        columns_of.append(hit)
    flipped[...] = jnp.concatenate(columns_of, axis=0).T[0:KC, :].astype(BF16)


def store_split(plane, z, high, low):
    top = plane.astype(BF16)
    high[z * CX : (z + 1) * CX, :] = top
    low[z * CX : (z + 1) * CX, :] = (plane - top.astype(F32)).astype(BF16)


def coarse_rows(high, low, flipped, factor, rows):
    hits = flipped[0:KC, :]
    sums = jnp.dot(hits, high[...], preferred_element_type=F32)
    sums = sums + jnp.dot(hits, low[...], preferred_element_type=F32)
    g_col = jnp.sum(sums[:, :LANES] + sums[:, LANES:], axis=1, keepdims=True)
    g = jnp.broadcast_to(g_col, (KC, LANES))
    factor = full(factor)
    for t in range(32):
        rows[t : t + 1, :] = jnp.sum(
            factor[:, t * LANES : (t + 1) * LANES] * g, axis=0, keepdims=True
        )
    return rows[...]


def face_blocks(field):
    return jnp.concatenate([field[0], field[1], field[CZ - 2], field[CZ - 1]], axis=0).astype(BF16)


def pack_body(ins, outs, tile, rows, wide, xs_lo, xs_hi, fhigh, flow):
    flags, label, zrow, r, factor, k = ins
    send, hits, flipped, put, take, *faces = outs
    label_hits(label, tile, raw(hits), raw(flipped))
    raw(put)[...], raw(take)[...] = zone_hits(full(zrow)[...])
    for x in (hits, flipped, put, take):
        x.send()
    for z in range(CZ):
        store_split(r[z], z, fhigh, flow)
    u_rows = coarse_rows(fhigh, flow, raw(flipped), factor, rows)
    store_send(raw(send), face_blocks(r), raw(put)[...], u_rows, (), tile, wide)
    send.send()
    face_store(lambda z: k[z], flags, faces, xs_lo, xs_hi)


def lift_store(out, wide, tail, zone):
    factor = zone[0]
    lane = iota((1, LANES), 1)
    u = jnp.where(lane < 32, tail + pltpu.roll(tail, LANES - 32, 1), 0.0)
    high = u.astype(BF16).astype(F32)
    both = high + pltpu.roll(u - high, 32, 1)
    size = ZN // WRITES
    for i in range(WRITES):
        at = i * size
        x = jnp.concatenate(
            [
                jnp.concatenate(
                    [wide[part_rows(k, at, size), :], wide[part_rows(CAP + k, at, size), :]],
                    axis=1,
                )
                for k in range(CAP)
            ],
            axis=0,
        ).astype(BF16)
        lifted = jnp.dot(x, factor, preferred_element_type=F32).astype(BF16)
        back = lax.dot_general(
            lifted, factor, (((1,), (1,)), ((), ())), preferred_element_type=F32
        )
        for k in range(CAP):
            rows = back[k * size : (k + 1) * size, :]
            wide[part_rows(k, at, size), :] = rows[:, :LANES]
            wide[part_rows(CAP + k, at, size), :] = rows[:, LANES:]
        wide[part_rows(EXTRA, at, size), :] = jnp.broadcast_to(both, (size, LANES))
        part = slice(at * PARTS, (at + size) * PARTS)
        out.buffer[part, :] = wide[part, :].astype(BF16)
        out.flush(i)


def tail_sum(wide):
    return jnp.sum(wide[part_rows(EXTRA), :], axis=0, keepdims=True)


def lift0_body(ins, outs, wide, sem):
    got, zone = ins
    out, kept = outs
    keep = pltpu.make_async_copy(got, kept, sem)
    keep.start()
    wide[...] = got[...].astype(F32)
    lift_store(out, wide, tail_sum(wide), full(zone))
    keep.wait()


def lift1_body(ins, outs, wide):
    zone, got0, got1 = ins
    out, scalars = outs
    store, scalars = scalars, raw(scalars)
    wide[...] = got1[...].astype(F32)
    tail1 = tail_sum(wide)
    lane = iota((1, LANES), 1)

    def scalar(i):
        keep = (lane >= 64 + 3 * i) & (lane < 67 + 3 * i)
        return jnp.sum(jnp.where(keep, tail1, 0.0), axis=1, keepdims=True)

    rz, curvature = scalar(0), scalar(1)
    alpha = rz / curvature
    scalars[0:1, :] = jnp.broadcast_to(alpha, (1, LANES))
    scalars[1:2, :] = jnp.broadcast_to(rz, (1, LANES))
    scalars[2:3, :] = jnp.broadcast_to(curvature, (1, LANES))
    scalars[3:8, :] = jnp.zeros((5, LANES), F32)
    store.send()
    wide[...] = full(got0)[...].astype(F32) - alpha * wide[...]
    lift_store(out, wide, tail_sum(wide), full(zone))


def minus_neighbours(p, below, above, cz_below, cz_above, cx, cy):
    tx = cx * p
    ty = cy * p
    out = p - cx * pltpu.roll(p, CX - 1, 0) - pltpu.roll(tx, 1, 0)
    out = out - cy * pltpu.roll(p, CY - 1, 1) - pltpu.roll(ty, 1, 1)
    if below is not None:
        out = out - cz_below * below
    if above is not None:
        out = out - cz_above * above
    return out


def cg(cz, cx, cy, s, p, q, e, y, first, local):
    def sweep(next_of, cz, cx, cy):
        rho = jnp.zeros((8, LANES), F32)
        pe, ee = rho, rho
        below, (now, left) = None, next_of(0)
        for z in range(CZ):
            rho = rho + fold(left * left)
            above = None
            if z + 1 < CZ:
                above, left = next_of(z + 1)
            image = minus_neighbours(
                now,
                below,
                above,
                cz[z - 1] if z else None,
                cz[z] if z + 1 < CZ else None,
                cx[z],
                cy[z],
            )
            e[z] = image
            pe = pe + fold(now * image)
            ee = ee + fold(image * image)
            below, now = now, above
        rho, pe, ee = total(rho), total(pe), total(ee)
        inverse = 1.0 / pe
        a = rho * inverse
        return a, a * ee * inverse - 1.0

    def begin(z):
        value = first(z)
        q[z] = value
        p[z] = value
        return value, value

    def second(a, beta):
        def next_of(z):
            old = p[z]
            y[z] = a * old
            left = q[z] - a * e[z]
            q[z] = left
            new = left + beta * old
            p[z] = new
            return new, left

        return next_of

    def later(a, beta):
        def next_of(z):
            old = p[z]
            y[z] = y[z] + a * old
            left = q[z] - a * e[z]
            q[z] = left
            new = left + beta * old
            p[z] = new
            return new, left

        return next_of

    carry = sweep(begin, cz, cx, cy)
    cz, cx, cy = full(cz), full(cx), full(cy)
    carry = sweep(second(*carry), cz, cx, cy)
    carry = lax.fori_loop(0, INNER - 2, lambda _, c: sweep(later(*c), cz, cx, cy), carry)
    a = carry[0]
    for z in range(CZ):
        local[z] = s[z] * (y[z] + a * p[z])


def solve0_body(ins, outs, p, q, e, y, ky):
    flags, *halos, k, storage, r = ins
    local, s, sinv, cz, cx, cy, bounds_zx, bounds_y = outs
    sub, lane = iota((CX, CY), 0), iota((CX, CY), 1)
    zl, zh, xl, xh, y_rows = halo_values(flags, halos)
    zl, zh, xl, xh = flags[0] * zl, flags[1] * zh, flags[2] * xl, flags[3] * xh
    y_flags = jnp.where(iota((8, LINES), 0) == 0, flags[4], flags[5])
    y_rows = y_flags * y_rows
    ky[...] = edge_field(y_rows)
    zx, by = raw(bounds_zx), raw(bounds_y)
    zx[0:32, :] = flags[0] * 0.5 * (k[0] + zl)
    planes = []
    for z in range(CZ):
        c = k[z]
        planes.append(c.astype(BF16))
        x_row_lo, x_row_hi = xl[z : z + 1, :], xh[z : z + 1, :]
        zx[64 + z : 65 + z, :] = flags[2] * 0.5 * (c[0:1, :] + x_row_lo)
        zx[80 + z : 81 + z, :] = flags[3] * 0.5 * (c[CX - 1 : CX, :] + x_row_hi)
        around = (k[z - 1] if z else zl) + (k[z + 1] if z + 1 < CZ else zh)
        right = pltpu.roll(c, CX - 1, 0)
        around = around + jnp.where(sub == CX - 1, x_row_hi, right)
        around = around + jnp.where(sub == 0, x_row_lo, pltpu.roll(c, 1, 0))
        ahead = pltpu.roll(c, CY - 1, 1)
        beyond = ky[z * CX : (z + 1) * CX, :]
        around = around + jnp.where(lane == CY - 1, beyond, ahead)
        around = around + jnp.where(lane == 0, beyond, pltpu.roll(c, 1, 1))
        diagonal = storage[z] + 3.0 * c + 0.5 * around
        root = lax.rsqrt(diagonal)
        root = root * (1.5 - 0.5 * diagonal * root * root)
        s[z] = root
        sinv[z] = diagonal * root
        cx[z] = jnp.where(sub == CX - 1, 0.0, 0.5 * (c + right) * root * pltpu.roll(root, CX - 1, 0))
        cy[z] = jnp.where(lane == CY - 1, 0.0, 0.5 * (c + ahead) * root * pltpu.roll(root, CY - 1, 1))
        if z:
            cz[z - 1] = 0.5 * (k[z - 1] + c) * s[z - 1] * root
    cz[CZ - 1] = jnp.zeros((CX, CY), F32)
    zx[32:64, :] = flags[1] * 0.5 * (k[CZ - 1] + zh)
    by[...] = y_flags * 0.5 * (edge_rows(jnp.concatenate(planes, axis=0)) + y_rows)
    bounds_zx.send()
    bounds_y.send()
    cg(raw(cz), raw(cx), raw(cy), raw(s), p, q, e, y, lambda z: s[z] * r[z], local)


def solve1_body(ins, outs, p, q, e, y):
    scalars, r, image, s, cz, cx, cy = ins
    (local,) = outs
    alpha = full(scalars)[0:1, 0:1]
    cg(cz, cx, cy, s, p, q, e, y, lambda z: s[z] * (r[z] - alpha * image[z]), local)


def combine_body(ins, outs, xs_lo, xs_hi, wide, lines):
    flags, got, factor, hits, take, local, *_ = ins
    out, *faces = outs
    wide[...] = got[...].astype(F32)
    factor = full(factor)
    flipped = wide[part_rows(EXTRA), :].T
    u = flipped[0:32, :] + flipped[32:64, :]
    acc = jnp.zeros((KC, LANES), F32)
    for t in range(32):
        acc = acc + factor[:, t * LANES : (t + 1) * LANES] * u[t : t + 1, :]
    coef_col = jnp.sum(acc, axis=1, keepdims=True)
    pieces = split3(jnp.broadcast_to(coef_col, (KC, CY)))
    coef = jnp.concatenate([*pieces, jnp.zeros((LANES - 3 * KC, CY), F32)], axis=0)
    lines[...] = jnp.dot(full(hits)[...], coef.astype(BF16), preferred_element_type=F32)
    back = jnp.concatenate(
        [
            jnp.concatenate([wide[part_rows(k), :], wide[part_rows(CAP + k), :]], axis=1)
            for k in range(CAP)
        ],
        axis=0,
    ).astype(BF16)
    placed = jnp.dot(full(take)[...], back, preferred_element_type=F32)
    order = {0: 0, 1: 1, CZ - 2: 2, CZ - 1: 3}
    for z in range(CZ):
        plane = local[z] + lines[z * CX : (z + 1) * CX, :]
        if z in order:
            at = order[z] * CX
            plane = plane + placed[at : at + CX, :]
        out[z] = plane
    face_store(lambda z: out[z], flags, faces, xs_lo, xs_hi)


def apply_layers(v, sinv, cz, cx, cy, zx, by, flags, halos, beyond):
    zl, zh, xl, xh, y_rows = halo_values(flags, halos)
    beyond[...] = edge_field(by[...] * y_rows)
    xl, xh = zx[64:80, :] * xl, zx[80:96, :] * xh
    sub = iota((CX, CY), 0)
    first_row, last_row = sub == 0, sub == CX - 1
    below, now = None, v[0] * sinv[0]
    for z in range(CZ):
        above = v[z + 1] * sinv[z + 1] if z + 1 < CZ else None
        scaled = minus_neighbours(
            now,
            below,
            above,
            cz[z - 1] if z else None,
            cz[z] if z + 1 < CZ else None,
            cx[z],
            cy[z],
        )
        out = scaled * sinv[z] - beyond[z * CX : (z + 1) * CX, :]
        row = jnp.where(first_row, xl[z : z + 1, :], 0.0)
        out = out - jnp.where(last_row, xh[z : z + 1, :], row)
        if z == 0:
            out = out - zx[0:32, :] * zl
        if z == CZ - 1:
            out = out - zx[32:64, :] * zh
        yield z, out
        below, now = now, above


def apply0_body(ins, outs, tile, rows, wide, beyond, fhigh, flow, sem):
    flags, v, sinv, cz, cx, cy, zx, by, r, *halos, flipped, put, factor = ins
    image, send, kept = outs
    keep = pltpu.make_async_copy(v, kept, sem)
    keep.start()
    rz = jnp.zeros((8, LANES), F32)
    curvature = jnp.zeros((8, LANES), F32)
    for z, out in apply_layers(v, sinv, cz, cx, cy, zx, by, flags, halos, beyond):
        image[z] = out
        store_split(out, z, fhigh, flow)
        rz = rz + fold(r[z] * v[z])
        curvature = curvature + fold(v[z] * out)
    u_rows = coarse_rows(fhigh, flow, full(flipped), factor, rows)
    sums = (total(rz), total(curvature))
    store_send(raw(send), face_blocks(image), full(put)[...], u_rows, sums, tile, wide)
    send.send()
    keep.wait()


def apply1_body(ins, outs, beyond, sem):
    flags, v, sinv, cz, cx, cy, zx, by, r, image0, *halos = ins
    image, sums, kept = outs
    keep = pltpu.make_async_copy(v, kept, sem)
    keep.start()
    sums3 = [jnp.zeros((8, LANES), F32) for _ in range(3)]
    for z, out in apply_layers(v, sinv, cz, cx, cy, zx, by, flags, halos, beyond):
        image[z] = out
        at = v[z]
        sums3[0] = sums3[0] + fold(r[z] * at)
        sums3[1] = sums3[1] + fold(at * out)
        sums3[2] = sums3[2] + fold(at * image0[z])
    lane = iota((ZN, LANES), 1)
    row = jnp.zeros((ZN, LANES), F32)
    for i in range(3):
        row = jnp.where(lane == i, total(sums3[i]), row)
    sums[...] = row
    keep.wait()


def final_body(ins, outs):
    scalars, got, d, v, r, image0, image1 = ins
    solution, residual = outs
    scalars = full(scalars)
    sums = jnp.sum(got[...], axis=0, keepdims=True)
    alpha0, rz0, curvature0 = scalars[0:1, 0:1], scalars[1:2, 0:1], scalars[2:3, 0:1]
    rv, vav, vad = sums[:, 0:1], sums[:, 1:2], sums[:, 2:3]
    rz1 = rv - alpha0 * vad
    beta = rz1 / rz0
    alpha1 = rz1 / (vav + 2.0 * beta * vad + beta * beta * curvature0)
    mix = alpha0 + alpha1 * beta
    for z in range(CZ):
        solution[z] = mix * d[z] + alpha1 * v[z]
        residual[z] = r[z] - mix * image0[z] - alpha1 * image1[z]


FIELD = sds((CZ, CX, CY))
FIELD_SCRATCH = pltpu.VMEM((CZ, CX, CY), F32)
PACKED = sds((ZN * PARTS, LANES), BF16)
WIDE = pltpu.VMEM((ZN * PARTS, LANES), F32)
TILE = pltpu.VMEM((LANES, LANES), F32)
ROWS = pltpu.VMEM((KC, LANES), F32)
LINE_FIELD = pltpu.VMEM((LINES, CY), F32)
HITS = sds((LINES, LANES), BF16)
FLIPPED = sds((KC, LINES), BF16)
FLAT = pltpu.VMEM((LINES, CY), BF16)
PUT = sds((CAP * ZN, ZN), BF16)
TAKE = sds((ZN, CAP * ZN), BF16)


def swap(x):
    return lax.all_to_all(x, AX, split_axis=0, concat_axis=0, tiled=True)


def swap_packed(x):
    return swap(x.reshape(ZN, PARTS // 2, 2, LANES)).reshape(ZN * PARTS, LANES)


def each(mode, *arrays):
    return [(mode, a) for a in arrays]


def per_device(r, storage, k, label, zone_of_block, factor, zone_factor):
    zrow = zone_of_block.reshape(1, ZN)
    label = label.reshape(CZ, CX)
    flags = jnp.stack(
        [
            (lax.axis_index(axis) != edge).astype(F32)
            for axis in ("gz", "gx", "gy")
            for edge in (0, lax.axis_size(axis) - 1)
        ]
        + [(1 - lax.axis_index(axis) % 2).astype(F32) for axis in ("gz", "gx", "gy")]
    )
    send0, hits, flipped, put, take, *k_faces = run(
        pack_body,
        each("s", flags) + each("h", label, zrow, r, factor, k),
        each("h", PACKED, HITS, FLIPPED, PUT, TAKE, *FACE_OUTS),
        (TILE, ROWS, WIDE) + FACE_SCRATCH + (FLAT, FLAT),
    )
    got0 = swap_packed(send0)
    k_halos = exchange(k_faces)
    got0, *k_halos = lax.optimization_barrier((got0, *k_halos))
    back0, got0 = run(
        lift0_body,
        each("v", got0) + each("h", zone_factor),
        each("w", PACKED) + each("o", PACKED),
        (WIDE, pltpu.SemaphoreType.DMA),
    )
    back0 = swap_packed(back0)
    local, s, sinv, cz, cx, cy, *bounds = run(
        solve0_body,
        each("s", flags) + each("a", *k_halos) + each("c", k, storage, r),
        each("w", FIELD) + each("h", *(FIELD,) * 5, sds((96, CY)), sds((8, LINES))),
        (FIELD_SCRATCH,) * 4 + (LINE_FIELD,),
        ((7, 8, 9),),
    )
    matrix = (sinv, cz, cx, cy, *bounds)

    def combine(local, back, more):
        field, *rest = run(
            combine_body,
            each("s", flags)
            + each("v", back)
            + each("h", factor, hits, take)
            + each("c", local)
            + each("p", *matrix, *more),
            each("v", FIELD, *FACE_OUTS),
            FACE_SCRATCH + (WIDE, LINE_FIELD),
        )
        return field, exchange(rest[:5]), rest[5:]

    field, halos, passed = combine(local, back0, (r,))
    image0, send1, d = run(
        apply0_body,
        each("s", flags) + each("v", field, *passed, *halos) + each("h", flipped, put, factor),
        each("h", FIELD, PACKED) + each("o", FIELD),
        (TILE, ROWS, WIDE, LINE_FIELD, FLAT, FLAT, pltpu.SemaphoreType.DMA),
    )
    got1 = swap_packed(send1)
    back1, scalars = run(
        lift1_body,
        each("h", zone_factor, got0) + each("v", got1),
        each("w", PACKED) + each("h", sds((8, LANES))),
        (WIDE,),
    )
    back1 = swap_packed(back1)
    (local,) = run(
        solve1_body,
        each("h", scalars) + each("c", r, image0, s, cz, cx, cy),
        each("w", FIELD),
        (FIELD_SCRATCH,) * 4,
        ((1, 2, 3), (4, 5, 6)),
    )
    field, halos, passed = combine(local, back1, (r, image0))
    image1, sums, v = run(
        apply1_body,
        each("s", flags) + each("v", field, *passed, *halos),
        each("w", FIELD) + each("v", sds((ZN, LANES))) + each("o", FIELD),
        (LINE_FIELD, pltpu.SemaphoreType.DMA),
    )
    return run(
        final_body,
        each("h", scalars) + each("v", swap(sums)) + each("c", d, v, r, image0, image1),
        each("w", FIELD, FIELD),
        (),
        ((2, 3, 4, 5, 6),),
    )


def solution(mesh):
    field = P("gz", "gx", "gy")
    in_specs = (field, field, field, field, P(AX, None), P(AX, None), P(AX, None, None))
    return jax.shard_map(
        per_device, mesh=mesh, in_specs=in_specs, out_specs=(field, field), check_vma=False
    )
```

```python
import jax
import jax.numpy as jnp
from jax import lax
from jax.experimental import pallas as pl
from jax.experimental.pallas import tpu as pltpu
from jax.sharding import PartitionSpec as P

CZ = 16
CX = 32
CY = 256
KC = 32
INNER = 8
CAP = 4
ZN = 128
FB = 256
EXTRA = 2 * CAP
PARTS = EXTRA + 2
LANES = 128
LINES = CZ * CX
AX = ("gx", "gy", "gz")
F32 = jnp.float32
BF16 = jnp.bfloat16

def sds(shape, dtype=F32):
    return jax.ShapeDtypeStruct(shape, dtype)


class Load:
    def __init__(self, source, buffer, sems, chunks):
        self.buffer = buffer
        self.size = buffer.shape[0] // chunks
        self.copies = []
        for i in range(chunks):
            part = pl.ds(i * self.size, self.size)
            self.copies.append(
                pltpu.make_async_copy(source.at[part], buffer.at[part], sems.at[i])
            )

    def start(self, i):
        self.copies[i].start()

    def wait(self, i):
        if self.copies[i] is not None:
            self.copies[i].wait()
            self.copies[i] = None

    def full(self):
        for i in range(len(self.copies)):
            self.wait(i)
        return self.buffer

    def __getitem__(self, z):
        self.wait(z // self.size)
        return self.buffer[z]


class Store:
    def __init__(self, target, buffer, sems, chunks):
        self.buffer, self.target, self.sems = buffer, target, sems
        self.size = buffer.shape[0] // chunks
        self.copies = [None] * chunks

    def flush(self, i):
        part = pl.ds(i * self.size, self.size)
        copy = pltpu.make_async_copy(self.buffer.at[part], self.target.at[part], self.sems.at[i])
        copy.start()
        self.copies[i] = copy

    def __setitem__(self, z, value):
        self.buffer[z] = value
        if z % self.size == self.size - 1:
            self.flush(z // self.size)

    def __getitem__(self, z):
        return self.buffer[z]

    def send(self):
        for i, copy in enumerate(self.copies):
            if copy is None:
                self.flush(i)

    def finish(self):
        self.send()
        for copy in self.copies:
            copy.wait()


SPACE = {"a": pl.ANY, "o": pltpu.HBM, "s": pltpu.SMEM, "v": pltpu.VMEM, "h": pltpu.HBM, "c": pltpu.HBM, "p": pltpu.HBM, "w": pltpu.HBM}
COPIED = "hcpaw"
CHUNKS = 2
WRITES = 2


def chunks_of(mode, array):
    return {"c": CHUNKS, "w": WRITES}.get(mode, 1)


def spec(mode):
    return pl.BlockSpec(memory_space=SPACE[mode])


def run(body, ins, outs, scratch=(), mixed=()):
    moved = [(m, a) for side in (ins, outs) for m, a in side if m in COPIED]
    n_chunks = [chunks_of(m, a) for m, a in moved]
    buffers = [pltpu.VMEM(a.shape, a.dtype) for m, a in moved if m != "p"]
    sems = [pltpu.SemaphoreType.DMA((n,)) for n in n_chunks]
    passed = [sds(a.shape, a.dtype) for m, a in ins if m == "p"]
    n_in, n_out, n_pass, n_own = len(ins), len(outs), len(passed), len(scratch)

    def kernel(*refs):
        refs = list(refs)

        def take(n):
            head = refs[:n]
            del refs[:n]
            return head

        in_refs, out_refs, pass_refs, own = take(n_in), take(n_out), take(n_pass), take(n_own)
        bufs = take(len(buffers))
        given, made, loads, stores = [], [], [], []
        for (m, _), ref in zip(ins, in_refs):
            if m in COPIED:
                buf = pass_refs.pop(0) if m == "p" else bufs.pop(0)
                given.append(Load(ref, buf, refs.pop(0), chunks_of(m, buf)))
                loads.append(given[-1])
            else:
                given.append(ref)
        for (m, _), ref in zip(outs, out_refs):
            if m in COPIED:
                made.append(Store(ref, bufs[0], refs.pop(0), chunks_of(m, bufs.pop(0))))
                stores.append(made[-1])
            else:
                made.append(ref)
        groups = {id(given[g[0]]): [given[i] for i in g] for g in mixed}
        joined = [id(given[i]) for g in mixed for i in g]
        for x in loads:
            for i in range(len(x.copies)):
                if id(x) not in joined:
                    x.start(i)
                for one in groups.get(id(x), ()):
                    one.start(i)
        body(given, made, *own)
        for x in stores:
            x.send()
        for x in loads:
            x.full()
        for x in stores:
            x.finish()

    return pl.pallas_call(
        kernel,
        out_shape=tuple(
            pltpu.HBM(a.shape, a.dtype) if m in "hcow" else a for m, a in outs
        )
        + tuple(passed),
        in_specs=[spec(m) for m, _ in ins],
        out_specs=tuple(spec(m) for m, _ in outs) + (spec("v"),) * n_pass,
        scratch_shapes=tuple(scratch) + tuple(buffers) + tuple(sems),
        compiler_params=pltpu.CompilerParams(vmem_limit_bytes=24 * 1024 * 1024),
    )(*[pltpu.with_memory_space_constraint(a, pltpu.HBM) if m in "hcp" else a for m, a in ins])


def full(x):
    return x.full() if isinstance(x, Load) else x


def raw(x):
    return x.buffer if isinstance(x, (Load, Store)) else x


def iota(shape, dim):
    return lax.broadcasted_iota(jnp.int32, shape, dim)


def total(x):
    return jnp.sum(jnp.sum(x, axis=1, keepdims=True), axis=0, keepdims=True)


def fold(x):
    half = x[:, :LANES] + x[:, LANES:]
    return half[0:8] + half[8:16] + half[16:24] + half[24:32]


def split3(x):
    high = x.astype(BF16).astype(F32)
    rest = x - high
    mid = rest.astype(BF16).astype(F32)
    return high, mid, rest - mid


def choose(even, first, second):
    return even * first + (1.0 - even) * second


def edge_rows(flat):
    shape = (8, CY)
    sub, lane = iota(shape, 0), iota(shape, 1)
    hit = ((sub == 0) & (lane == 0)) | ((sub == 1) & (lane == CY - 1))
    pick = jnp.where(hit, 1.0, 0.0).astype(BF16)
    return lax.dot_general(pick, flat, (((1,), (1,)), ((), ())), preferred_element_type=F32)


def edge_field(rows):
    high, mid, low = split3(rows)
    sub = iota(rows.shape, 0)
    stack = jnp.where(
        sub < 2, high, jnp.where(sub < 4, pltpu.roll(mid, 2, 0), pltpu.roll(low, 4, 0))
    )
    shape = (8, CY)
    sub, lane = iota(shape, 0), iota(shape, 1)
    hit = ((sub % 2 == 0) & (lane == 0)) | ((sub % 2 == 1) & (lane == CY - 1))
    put = jnp.where(hit & (sub < 6), 1.0, 0.0).astype(BF16)
    stack = jnp.where(iota(rows.shape, 0) < 6, stack, 0.0)
    return jnp.dot(stack.T.astype(BF16), put, preferred_element_type=F32)


def face_store(plane_of, flags, refs, xs_lo, xs_hi):
    za, zb, xa, xb, ys = (raw(x) for x in refs)
    low, high = plane_of(0), plane_of(CZ - 1)
    za[...] = choose(flags[6], high, low).astype(BF16)
    zb[...] = choose(flags[6], low, high).astype(BF16)
    planes = []
    for z in range(CZ):
        plane = plane_of(z)
        xs_lo[z : z + 1, :] = plane[0:1, :]
        xs_hi[z : z + 1, :] = plane[CX - 1 : CX, :]
        planes.append(plane.astype(BF16))
    xa[...] = choose(flags[7], xs_hi[...], xs_lo[...]).astype(BF16)
    xb[...] = choose(flags[7], xs_lo[...], xs_hi[...]).astype(BF16)
    ys[...] = edge_rows(jnp.concatenate(planes, axis=0)).astype(BF16)


FACE_OUTS = (
    sds((CX, CY), BF16),
    sds((CX, CY), BF16),
    sds((CZ, CY), BF16),
    sds((CZ, CY), BF16),
    sds((8, LINES), BF16),
)
FACE_SCRATCH = (pltpu.VMEM((CZ, CY), F32), pltpu.VMEM((CZ, CY), F32))


def pair(axis, first, second):
    n = lax.axis_size(axis)
    even = [(i, i ^ 1) for i in range(n)]
    odd = [(i, (i + 1 if i % 2 else i - 1) % n) for i in range(n)]
    return [lax.ppermute(first, axis, even), lax.ppermute(second, axis, odd)]


def exchange(faces):
    za, zb, xa, xb, ys = faces
    return pair("gz", za, zb) + pair("gx", xa, xb) + pair("gy", ys, ys)


def halo_values(flags, got):
    za, zb, xa, xb, ya, yb = (full(x)[...].astype(F32) for x in got)
    low, high = choose(flags[8], yb, ya), choose(flags[8], ya, yb)
    shape = (8, LINES)
    sub = iota(shape, 0)
    rows = jnp.where(
        sub == 0,
        jnp.broadcast_to(low[1:2, :], shape),
        jnp.where(sub == 1, jnp.broadcast_to(high[0:1, :], shape), 0.0),
    )
    return (
        choose(flags[6], zb, za),
        choose(flags[6], za, zb),
        choose(flags[7], xb, xa),
        choose(flags[7], xa, xb),
        rows,
    )


def slots(zrow):
    shape = (ZN, ZN)
    sub, lane = iota(shape, 0), iota(shape, 1)
    row = jnp.broadcast_to(zrow, shape)
    zcol = jnp.sum(jnp.where(sub == lane, row, 0), axis=1, keepdims=True)
    same = row == zcol
    slot_row = jnp.sum(jnp.where(same & (sub < lane), 1, 0), axis=0, keepdims=True)
    slot_col = jnp.sum(jnp.where(same & (lane < sub), 1, 0), axis=1, keepdims=True)
    return zrow + ZN * slot_row, zcol + ZN * slot_col


def part_rows(part, first=0, count=ZN):
    return pl.ds(first * PARTS + part, count, stride=PARTS)


def zone_hits(zrow):
    row, col = slots(zrow)
    put = jnp.where(iota((CAP * ZN, ZN), 0) == row, 1.0, 0.0).astype(BF16)
    take = jnp.where(iota((ZN, CAP * ZN), 1) == col, 1.0, 0.0).astype(BF16)
    return put, take


def store_send(send, blocks, put, u_rows, scalars, tile, wide):
    placed = jnp.dot(put, blocks, preferred_element_type=F32)
    for k in range(CAP):
        rows = placed[k * ZN : (k + 1) * ZN, :]
        wide[part_rows(k), :] = rows[:, :LANES]
        wide[part_rows(CAP + k), :] = rows[:, LANES:]
    high = u_rows.astype(BF16).astype(F32)
    tile[0:32, :] = high
    tile[32:64, :] = u_rows - high
    tile[64:128, :] = jnp.zeros((64, LANES), F32)
    for i, value in enumerate(scalars):
        for j, piece in enumerate(split3(value)):
            at = 64 + 3 * i + j
            tile[at : at + 1, :] = jnp.broadcast_to(piece, (1, LANES))
    wide[part_rows(EXTRA), :] = tile[...].T
    wide[part_rows(EXTRA + 1), :] = jnp.zeros((ZN, LANES), F32)
    send[...] = wide[...].astype(BF16)


def label_hits(label, tile, hits, flipped):
    tile[...] = jnp.zeros((LANES, LANES), F32)
    tile[0:CZ, 0:CX] = full(label)[...].astype(F32)
    columns = tile[...].T[0:CX, :]
    lane = iota((CX, LANES), 1)
    kind = jnp.where(lane < 3 * KC, lane % KC, -1).astype(F32)
    columns_of = []
    for z in range(CZ):
        hit = jnp.where(columns[:, z : z + 1] == kind, 1.0, 0.0)
        hits[z * CX : (z + 1) * CX, :] = hit.astype(BF16)
        columns_of.append(hit)
    flipped[...] = jnp.concatenate(columns_of, axis=0).T[0:KC, :].astype(BF16)


def store_split(plane, z, high, low):
    top = plane.astype(BF16)
    high[z * CX : (z + 1) * CX, :] = top
    low[z * CX : (z + 1) * CX, :] = (plane - top.astype(F32)).astype(BF16)


def coarse_rows(high, low, flipped, factor, rows):
    hits = flipped[0:KC, :]
    sums = jnp.dot(hits, high[...], preferred_element_type=F32)
    sums = sums + jnp.dot(hits, low[...], preferred_element_type=F32)
    g_col = jnp.sum(sums[:, :LANES] + sums[:, LANES:], axis=1, keepdims=True)
    g = jnp.broadcast_to(g_col, (KC, LANES))
    factor = full(factor)
    for t in range(32):
        rows[t : t + 1, :] = jnp.sum(
            factor[:, t * LANES : (t + 1) * LANES] * g, axis=0, keepdims=True
        )
    return rows[...]


def face_blocks(field):
    return jnp.concatenate([field[0], field[1], field[CZ - 2], field[CZ - 1]], axis=0).astype(BF16)


def pack_body(ins, outs, tile, rows, wide, xs_lo, xs_hi, fhigh, flow):
    flags, label, zrow, r, factor, k = ins
    send, hits, flipped, put, take, *faces = outs
    label_hits(label, tile, raw(hits), raw(flipped))
    raw(put)[...], raw(take)[...] = zone_hits(full(zrow)[...])
    for x in (hits, flipped, put, take):
        x.send()
    for z in range(CZ):
        store_split(r[z], z, fhigh, flow)
    u_rows = coarse_rows(fhigh, flow, raw(flipped), factor, rows)
    store_send(raw(send), face_blocks(r), raw(put)[...], u_rows, (), tile, wide)
    send.send()
    face_store(lambda z: k[z], flags, faces, xs_lo, xs_hi)


def lift_store(out, wide, tail, zone):
    factor = zone[0]
    lane = iota((1, LANES), 1)
    u = jnp.where(lane < 32, tail + pltpu.roll(tail, LANES - 32, 1), 0.0)
    high = u.astype(BF16).astype(F32)
    both = high + pltpu.roll(u - high, 32, 1)
    size = ZN // WRITES
    for i in range(WRITES):
        at = i * size
        x = jnp.concatenate(
            [
                jnp.concatenate(
                    [wide[part_rows(k, at, size), :], wide[part_rows(CAP + k, at, size), :]],
                    axis=1,
                )
                for k in range(CAP)
            ],
            axis=0,
        ).astype(BF16)
        lifted = jnp.dot(x, factor, preferred_element_type=F32).astype(BF16)
        back = lax.dot_general(
            lifted, factor, (((1,), (1,)), ((), ())), preferred_element_type=F32
        )
        for k in range(CAP):
            rows = back[k * size : (k + 1) * size, :]
            wide[part_rows(k, at, size), :] = rows[:, :LANES]
            wide[part_rows(CAP + k, at, size), :] = rows[:, LANES:]
        wide[part_rows(EXTRA, at, size), :] = jnp.broadcast_to(both, (size, LANES))
        part = slice(at * PARTS, (at + size) * PARTS)
        out.buffer[part, :] = wide[part, :].astype(BF16)
        out.flush(i)


def tail_sum(wide):
    return jnp.sum(wide[part_rows(EXTRA), :], axis=0, keepdims=True)


def lift0_body(ins, outs, wide, sem):
    got, zone = ins
    out, kept = outs
    keep = pltpu.make_async_copy(got, kept, sem)
    keep.start()
    wide[...] = got[...].astype(F32)
    lift_store(out, wide, tail_sum(wide), full(zone))
    keep.wait()


def lift1_body(ins, outs, wide):
    zone, got0, got1 = ins
    out, scalars = outs
    store, scalars = scalars, raw(scalars)
    wide[...] = got1[...].astype(F32)
    tail1 = tail_sum(wide)
    lane = iota((1, LANES), 1)

    def scalar(i):
        keep = (lane >= 64 + 3 * i) & (lane < 67 + 3 * i)
        return jnp.sum(jnp.where(keep, tail1, 0.0), axis=1, keepdims=True)

    rz, curvature = scalar(0), scalar(1)
    alpha = rz / curvature
    scalars[0:1, :] = jnp.broadcast_to(alpha, (1, LANES))
    scalars[1:2, :] = jnp.broadcast_to(rz, (1, LANES))
    scalars[2:3, :] = jnp.broadcast_to(curvature, (1, LANES))
    scalars[3:8, :] = jnp.zeros((5, LANES), F32)
    store.send()
    wide[...] = full(got0)[...].astype(F32) - alpha * wide[...]
    lift_store(out, wide, tail_sum(wide), full(zone))


def minus_neighbours(p, below, above, cz_below, cz_above, cx, cy):
    tx = cx * p
    ty = cy * p
    out = p - cx * pltpu.roll(p, CX - 1, 0) - pltpu.roll(tx, 1, 0)
    out = out - cy * pltpu.roll(p, CY - 1, 1) - pltpu.roll(ty, 1, 1)
    if below is not None:
        out = out - cz_below * below
    if above is not None:
        out = out - cz_above * above
    return out


def cg(cz, cx, cy, s, p, q, e, y, first, local):
    def sweep(next_of, cz, cx, cy, last=False):
        rho = jnp.zeros((8, LANES), F32)
        pe, ee = rho, rho
        below, (now, left) = None, next_of(0)
        for z in range(CZ):
            rho = rho + fold(left * left)
            above = None
            if z + 1 < CZ:
                above, left = next_of(z + 1)
            image = minus_neighbours(
                now,
                below,
                above,
                cz[z - 1] if z else None,
                cz[z] if z + 1 < CZ else None,
                cx[z],
                cy[z],
            )
            pe = pe + fold(now * image)
            if not last:
                e[z] = image
                ee = ee + fold(image * image)
            below, now = now, above
        rho, pe = total(rho), total(pe)
        if last:
            return rho / pe
        ee = total(ee)
        inverse = 1.0 / pe
        a = rho * inverse
        return a, a * ee * inverse - 1.0

    def begin(z):
        value = first(z)
        q[z] = value
        p[z] = value
        return value, value

    def second(a, beta):
        def next_of(z):
            old = p[z]
            y[z] = a * old
            left = q[z] - a * e[z]
            q[z] = left
            new = left + beta * old
            p[z] = new
            return new, left

        return next_of

    def later(a, beta, last=False):
        def next_of(z):
            old = p[z]
            y[z] = y[z] + a * old
            left = q[z] - a * e[z]
            if not last:
                q[z] = left
            new = left + beta * old
            p[z] = new
            return new, left

        return next_of

    carry = sweep(begin, cz, cx, cy)
    cz, cx, cy = full(cz), full(cx), full(cy)
    carry = sweep(second(*carry), cz, cx, cy)
    carry = lax.fori_loop(0, INNER - 3, lambda _, c: sweep(later(*c), cz, cx, cy), carry)
    a = sweep(later(*carry, last=True), cz, cx, cy, last=True)
    for z in range(CZ):
        local[z] = s[z] * (y[z] + a * p[z])


def solve0_body(ins, outs, p, q, e, y, ky):
    flags, *halos, k, storage, r = ins
    local, s, sinv, cz, cx, cy, bounds_zx, bounds_y = outs
    sub, lane = iota((CX, CY), 0), iota((CX, CY), 1)
    zl, zh, xl, xh, y_rows = halo_values(flags, halos)
    zl, zh, xl, xh = flags[0] * zl, flags[1] * zh, flags[2] * xl, flags[3] * xh
    y_flags = jnp.where(iota((8, LINES), 0) == 0, flags[4], flags[5])
    y_rows = y_flags * y_rows
    ky[...] = edge_field(y_rows)
    zx, by = raw(bounds_zx), raw(bounds_y)
    zx[0:32, :] = flags[0] * 0.5 * (k[0] + zl)
    planes = []
    for z in range(CZ):
        c = k[z]
        planes.append(c.astype(BF16))
        x_row_lo, x_row_hi = xl[z : z + 1, :], xh[z : z + 1, :]
        zx[64 + z : 65 + z, :] = flags[2] * 0.5 * (c[0:1, :] + x_row_lo)
        zx[80 + z : 81 + z, :] = flags[3] * 0.5 * (c[CX - 1 : CX, :] + x_row_hi)
        around = (k[z - 1] if z else zl) + (k[z + 1] if z + 1 < CZ else zh)
        right = pltpu.roll(c, CX - 1, 0)
        around = around + jnp.where(sub == CX - 1, x_row_hi, right)
        around = around + jnp.where(sub == 0, x_row_lo, pltpu.roll(c, 1, 0))
        ahead = pltpu.roll(c, CY - 1, 1)
        beyond = ky[z * CX : (z + 1) * CX, :]
        around = around + jnp.where(lane == CY - 1, beyond, ahead)
        around = around + jnp.where(lane == 0, beyond, pltpu.roll(c, 1, 1))
        diagonal = storage[z] + 3.0 * c + 0.5 * around
        root = lax.rsqrt(diagonal)
        root = root * (1.5 - 0.5 * diagonal * root * root)
        s[z] = root
        sinv[z] = diagonal * root
        cx[z] = jnp.where(sub == CX - 1, 0.0, 0.5 * (c + right) * root * pltpu.roll(root, CX - 1, 0))
        cy[z] = jnp.where(lane == CY - 1, 0.0, 0.5 * (c + ahead) * root * pltpu.roll(root, CY - 1, 1))
        if z:
            cz[z - 1] = 0.5 * (k[z - 1] + c) * s[z - 1] * root
    cz[CZ - 1] = jnp.zeros((CX, CY), F32)
    zx[32:64, :] = flags[1] * 0.5 * (k[CZ - 1] + zh)
    by[...] = y_flags * 0.5 * (edge_rows(jnp.concatenate(planes, axis=0)) + y_rows)
    bounds_zx.send()
    bounds_y.send()
    cg(raw(cz), raw(cx), raw(cy), raw(s), p, q, e, y, lambda z: s[z] * r[z], local)


def solve1_body(ins, outs, p, q, e, y):
    scalars, r, image, s, cz, cx, cy = ins
    (local,) = outs
    alpha = full(scalars)[0:1, 0:1]
    cg(cz, cx, cy, s, p, q, e, y, lambda z: s[z] * (r[z] - alpha * image[z]), local)


def combine_body(ins, outs, xs_lo, xs_hi, wide, lines):
    flags, got, factor, hits, take, local, *_ = ins
    out, *faces = outs
    wide[...] = got[...].astype(F32)
    factor = full(factor)
    flipped = wide[part_rows(EXTRA), :].T
    u = flipped[0:32, :] + flipped[32:64, :]
    acc = jnp.zeros((KC, LANES), F32)
    for t in range(32):
        acc = acc + factor[:, t * LANES : (t + 1) * LANES] * u[t : t + 1, :]
    coef_col = jnp.sum(acc, axis=1, keepdims=True)
    pieces = split3(jnp.broadcast_to(coef_col, (KC, CY)))
    coef = jnp.concatenate([*pieces, jnp.zeros((LANES - 3 * KC, CY), F32)], axis=0)
    lines[...] = jnp.dot(full(hits)[...], coef.astype(BF16), preferred_element_type=F32)
    back = jnp.concatenate(
        [
            jnp.concatenate([wide[part_rows(k), :], wide[part_rows(CAP + k), :]], axis=1)
            for k in range(CAP)
        ],
        axis=0,
    ).astype(BF16)
    placed = jnp.dot(full(take)[...], back, preferred_element_type=F32)
    order = {0: 0, 1: 1, CZ - 2: 2, CZ - 1: 3}
    for z in range(CZ):
        plane = local[z] + lines[z * CX : (z + 1) * CX, :]
        if z in order:
            at = order[z] * CX
            plane = plane + placed[at : at + CX, :]
        out[z] = plane
    face_store(lambda z: out[z], flags, faces, xs_lo, xs_hi)


def apply_layers(v, sinv, cz, cx, cy, zx, by, flags, halos, beyond):
    zl, zh, xl, xh, y_rows = halo_values(flags, halos)
    beyond[...] = edge_field(by[...] * y_rows)
    xl, xh = zx[64:80, :] * xl, zx[80:96, :] * xh
    sub = iota((CX, CY), 0)
    first_row, last_row = sub == 0, sub == CX - 1
    below, now = None, v[0] * sinv[0]
    for z in range(CZ):
        above = v[z + 1] * sinv[z + 1] if z + 1 < CZ else None
        scaled = minus_neighbours(
            now,
            below,
            above,
            cz[z - 1] if z else None,
            cz[z] if z + 1 < CZ else None,
            cx[z],
            cy[z],
        )
        out = scaled * sinv[z] - beyond[z * CX : (z + 1) * CX, :]
        row = jnp.where(first_row, xl[z : z + 1, :], 0.0)
        out = out - jnp.where(last_row, xh[z : z + 1, :], row)
        if z == 0:
            out = out - zx[0:32, :] * zl
        if z == CZ - 1:
            out = out - zx[32:64, :] * zh
        yield z, out
        below, now = now, above


def apply0_body(ins, outs, tile, rows, wide, beyond, fhigh, flow, sem):
    flags, v, sinv, cz, cx, cy, zx, by, r, *halos, flipped, put, factor = ins
    image, send, kept = outs
    keep = pltpu.make_async_copy(v, kept, sem)
    keep.start()
    rz = jnp.zeros((8, LANES), F32)
    curvature = jnp.zeros((8, LANES), F32)
    for z, out in apply_layers(v, sinv, cz, cx, cy, zx, by, flags, halos, beyond):
        image[z] = out
        store_split(out, z, fhigh, flow)
        rz = rz + fold(r[z] * v[z])
        curvature = curvature + fold(v[z] * out)
    u_rows = coarse_rows(fhigh, flow, full(flipped), factor, rows)
    sums = (total(rz), total(curvature))
    store_send(raw(send), face_blocks(image), full(put)[...], u_rows, sums, tile, wide)
    send.send()
    keep.wait()


def apply1_body(ins, outs, beyond, sem):
    flags, v, sinv, cz, cx, cy, zx, by, r, image0, *halos = ins
    image, sums, kept = outs
    keep = pltpu.make_async_copy(v, kept, sem)
    keep.start()
    sums3 = [jnp.zeros((8, LANES), F32) for _ in range(3)]
    for z, out in apply_layers(v, sinv, cz, cx, cy, zx, by, flags, halos, beyond):
        image[z] = out
        at = v[z]
        sums3[0] = sums3[0] + fold(r[z] * at)
        sums3[1] = sums3[1] + fold(at * out)
        sums3[2] = sums3[2] + fold(at * image0[z])
    lane = iota((ZN, LANES), 1)
    row = jnp.zeros((ZN, LANES), F32)
    for i in range(3):
        row = jnp.where(lane == i, total(sums3[i]), row)
    sums[...] = row
    keep.wait()


def final_body(ins, outs):
    scalars, got, d, v, r, image0, image1 = ins
    solution, residual = outs
    scalars = full(scalars)
    sums = jnp.sum(got[...], axis=0, keepdims=True)
    alpha0, rz0, curvature0 = scalars[0:1, 0:1], scalars[1:2, 0:1], scalars[2:3, 0:1]
    rv, vav, vad = sums[:, 0:1], sums[:, 1:2], sums[:, 2:3]
    rz1 = rv - alpha0 * vad
    beta = rz1 / rz0
    alpha1 = rz1 / (vav + 2.0 * beta * vad + beta * beta * curvature0)
    mix = alpha0 + alpha1 * beta
    for z in range(CZ):
        solution[z] = mix * d[z] + alpha1 * v[z]
        residual[z] = r[z] - mix * image0[z] - alpha1 * image1[z]


FIELD = sds((CZ, CX, CY))
FIELD_SCRATCH = pltpu.VMEM((CZ, CX, CY), F32)
PACKED = sds((ZN * PARTS, LANES), BF16)
WIDE = pltpu.VMEM((ZN * PARTS, LANES), F32)
TILE = pltpu.VMEM((LANES, LANES), F32)
ROWS = pltpu.VMEM((KC, LANES), F32)
LINE_FIELD = pltpu.VMEM((LINES, CY), F32)
HITS = sds((LINES, LANES), BF16)
FLIPPED = sds((KC, LINES), BF16)
FLAT = pltpu.VMEM((LINES, CY), BF16)
PUT = sds((CAP * ZN, ZN), BF16)
TAKE = sds((ZN, CAP * ZN), BF16)


def swap(x):
    return lax.all_to_all(x, AX, split_axis=0, concat_axis=0, tiled=True)


def swap_packed(x):
    return swap(x.reshape(ZN, PARTS // 2, 2, LANES)).reshape(ZN * PARTS, LANES)


def each(mode, *arrays):
    return [(mode, a) for a in arrays]


def per_device(r, storage, k, label, zone_of_block, factor, zone_factor):
    zrow = zone_of_block.reshape(1, ZN)
    label = label.reshape(CZ, CX)
    flags = jnp.stack(
        [
            (lax.axis_index(axis) != edge).astype(F32)
            for axis in ("gz", "gx", "gy")
            for edge in (0, lax.axis_size(axis) - 1)
        ]
        + [(1 - lax.axis_index(axis) % 2).astype(F32) for axis in ("gz", "gx", "gy")]
    )
    send0, hits, flipped, put, take, *k_faces = run(
        pack_body,
        each("s", flags) + each("h", label, zrow, r, factor, k),
        each("h", PACKED, HITS, FLIPPED, PUT, TAKE, *FACE_OUTS),
        (TILE, ROWS, WIDE) + FACE_SCRATCH + (FLAT, FLAT),
    )
    got0 = swap_packed(send0)
    k_halos = exchange(k_faces)
    got0, *k_halos = lax.optimization_barrier((got0, *k_halos))
    back0, got0 = run(
        lift0_body,
        each("v", got0) + each("h", zone_factor),
        each("w", PACKED) + each("o", PACKED),
        (WIDE, pltpu.SemaphoreType.DMA),
    )
    back0 = swap_packed(back0)
    local, s, sinv, cz, cx, cy, *bounds = run(
        solve0_body,
        each("s", flags) + each("a", *k_halos) + each("c", k, storage, r),
        each("w", FIELD) + each("h", *(FIELD,) * 5, sds((96, CY)), sds((8, LINES))),
        (FIELD_SCRATCH,) * 4 + (LINE_FIELD,),
        ((7, 8, 9),),
    )
    matrix = (sinv, cz, cx, cy, *bounds)

    def combine(local, back, more):
        field, *rest = run(
            combine_body,
            each("s", flags)
            + each("v", back)
            + each("h", factor, hits, take)
            + each("c", local)
            + each("p", *matrix, *more),
            each("v", FIELD, *FACE_OUTS),
            FACE_SCRATCH + (WIDE, LINE_FIELD),
        )
        return field, exchange(rest[:5]), rest[5:]

    field, halos, passed = combine(local, back0, (r,))
    image0, send1, d = run(
        apply0_body,
        each("s", flags) + each("v", field, *passed, *halos) + each("h", flipped, put, factor),
        each("h", FIELD, PACKED) + each("o", FIELD),
        (TILE, ROWS, WIDE, LINE_FIELD, FLAT, FLAT, pltpu.SemaphoreType.DMA),
    )
    got1 = swap_packed(send1)
    back1, scalars = run(
        lift1_body,
        each("h", zone_factor, got0) + each("v", got1),
        each("w", PACKED) + each("h", sds((8, LANES))),
        (WIDE,),
    )
    back1 = swap_packed(back1)
    (local,) = run(
        solve1_body,
        each("h", scalars) + each("c", r, image0, s, cz, cx, cy),
        each("w", FIELD),
        (FIELD_SCRATCH,) * 4,
        ((1, 2, 3), (4, 5, 6)),
    )
    field, halos, passed = combine(local, back1, (r, image0))
    image1, sums, v = run(
        apply1_body,
        each("s", flags) + each("v", field, *passed, *halos),
        each("w", FIELD) + each("v", sds((ZN, LANES))) + each("o", FIELD),
        (LINE_FIELD, pltpu.SemaphoreType.DMA),
    )
    return run(
        final_body,
        each("h", scalars) + each("v", swap(sums)) + each("c", d, v, r, image0, image1),
        each("w", FIELD, FIELD),
        (),
        ((2, 3, 4, 5, 6),),
    )


def solution(mesh):
    field = P("gz", "gx", "gy")
    in_specs = (field, field, field, field, P(AX, None), P(AX, None), P(AX, None, None))
    return jax.shard_map(
        per_device, mesh=mesh, in_specs=in_specs, out_specs=(field, field), check_vma=False
    )
```
